32 devices in a mesh: dom: 32 (over z, y, x, core).
Axes of the slice: x: 2, y: 2, z: 4, core: 2. Of those that a mesh axis runs over, the one named last changes fastest.
Arguments:
- feats: bfloat16 [196608, 128], P('dom'), may hold values from -6 to 6
- adj_vals: bfloat16 [1536, 4, 128, 128], P('dom'), may hold values from 0.0099487305 to 0.099609375
- adj_cols: int32 [1536, 4], P('dom'), may hold values from 0 to 47
- hub_feats: bfloat16 [2048, 128], P('dom'), may hold values from -6 to 6
- hub_mirrors: int32 [2048, 8], P('dom'), may hold values from 0 to 31, all different within a row; in each aligned block of 64 rows (0 to 63, 64 to 127, ...) at most 32 rows name the same one
- hub_links: int32 [2048, 8, 8], P('dom'), may hold values from 0 to 6143
- labels: int32 [196608], P('dom'), may hold values from 0 to 171
- groups: int32 [196608], P('dom'), may hold values from 0 to 63
- train_mask: int32 [196608], P('dom'), may hold values 0 or 1
- w_self: bfloat16 [128, 512], replicated, may hold values from -0.5 to 0.5
- w_neigh: bfloat16 [128, 512], replicated, may hold values from -0.5 to 0.5
- bias: float32 [512], replicated, may hold values from -3 to 3
- w_cls: bfloat16 [512, 172], replicated, may hold values from -40 to 40
- group_logw: float32 [64], replicated, may hold values from -4 to 154
Outputs:
- objective: float32 [], replicated
- grad_w_self: float32 [128, 512], replicated
- grad_w_neigh: float32 [128, 512], replicated
- grad_bias: float32 [512], replicated
- grad_w_cls: float32 [512, 172], replicated
- hub_grad: float32 [2048, 128], P('dom')
The draws below stay inside these ranges and needn't reach their ends.
Inputs may be any that keep to these rules, and one draw needn't show every extreme that they name: `hub_mirrors`: the 8 mirrors of a hub are distinct partitions. Among the 64 hubs of one owner no partition is named by more than 32 hubs, a bound that some block reaches.
All inputs are finite; a program needn't handle non-finite values. No bound on the sum of `train_mask` on one device may be relied on, other than what follows from the above.
Results may differ from the reference program's by a relative error of at most 0.012.
The reference program's roundings to bfloat16 on the way (of `agg`, `hidden`, `dlogits` and `dpre`) count: a program that leaves them out, or rounds other values in their place, can miss the bound.
Values may be sent and summed in bfloat16 or wider, within the bound.
No kernel may reach another device: no remote copies, remote signals or barrier semaphores. Data moves between devices by JAX's collectives and lax.ppermute only.
A program may use at most 128 MiB of HBM per device.

```python
import math
import jax
import jax.numpy as jnp
import numpy as np
from jax import lax

F = 128
H = 512
C = 172
TILE = 128
TPR = 4
V_DEV = 6144
HUB_DEV = 64
MIRRORS = 8
LINKS = 8
GROUPS = 64
CAP = 32
ROWBLK = 48
VERT = 196608
HUBS = 2048
N_DOM = 32


def draw_w_cls(key, part):
    first = jax.random.fold_in(key, 0)
    base = jnp.clip(jax.random.normal(first, (H, C), jnp.float32), -4.0, 4.0) * H ** (-0.5)
    return base.astype(jnp.bfloat16)


def draw_group_logw(key, part):
    first = jax.random.fold_in(key, 0)
    return jnp.clip(jax.random.normal(first, (GROUPS,), jnp.float32), -4.0, 4.0)


def set_ends(values, stream_key, smallest, high):
    spot = [jax.random.randint(jax.random.fold_in(stream_key, axis), (), 0, length) for axis, length in enumerate(values.shape)]
    main_axis = values.shape.index(max(values.shape))
    beside = spot[:main_axis] + [(spot[main_axis] + 1) % values.shape[main_axis]] + spot[main_axis + 1:]
    return values.at[tuple(spot)].set(smallest).at[tuple(beside)].set(high)


def shard_levels(own_key, shape, cuts, least, top_value):
    gain, own = 1.0, jax.random.fold_in(own_key, 6)
    for position, shards_of in cuts:
        steps = jnp.exp(jax.random.uniform(jax.random.fold_in(own, position), (shards_of,), jnp.float32, least / len(cuts), top_value / len(cuts)))
        gain = gain * jnp.repeat(steps, shape[position] // shards_of).reshape([-1 if axis == position else 1 for axis in range(len(shape))])
    return gain


def cumulative_ranks(number_of, slope):
    loads = [(1 << 20) // math.isqrt(grade ** slope) + 1 for grade in range(1, number_of + 1)]
    width = 1 + sum(loads) // (1 << 30)
    return np.cumsum(np.array([max(1, weight // width) for weight in loads]))


def ranked(stream_key, shape, count, skew):
    table = cumulative_ranks(count, skew)
    ticket = jax.random.randint(jax.random.fold_in(stream_key, 1), shape, 0, int(table[count - 1]))
    rank = jnp.searchsorted(jnp.asarray(table, jnp.int32), ticket, side="right")
    return jax.random.permutation(jax.random.fold_in(stream_key, 2), count)[rank].astype(jnp.int32)


def shared_out(own_key, own, number, rows, amount, top, bound, skew):
    ranking = jax.random.permutation(own_key, amount)
    crowded, usual = portions_of(amount, rows * top, bound, skew, True), portions_of(amount, rows * top, bound, skew, False)
    places = jnp.arange(amount)

    def named(tallies, rotation):
        used = int((tallies > 0).sum())
        fixed = max(1, used // 4)
        moved = fixed + (places - fixed + rotation * (used - fixed)) % max(1, amount - fixed)
        return jnp.zeros((amount,), jnp.int32).at[ranking[jnp.where(places < fixed, places, moved)]].set(jnp.asarray(tallies, jnp.int32))

    tallies = jnp.where(number % 4 == 0, named(crowded, number // 4), named(usual, number - number // 4 - 1))
    mixed = jax.random.permutation(jax.random.fold_in(own, 3), amount)
    giver, receiver = mixed[0:amount // 2 * 2:2], mixed[1:amount // 2 * 2:2]
    room = jnp.minimum(tallies[giver] - 1, bound - tallies[receiver]) // 2
    room = jnp.where((giver == ranking[0]) | (receiver == ranking[0]) | (tallies[receiver] == 0), 0, jnp.maximum(room, 0))
    moved = jax.random.randint(jax.random.fold_in(own, 4), (amount // 2,), 0, 1 << 20) % (room + 1)
    tallies = tallies.at[giver].add(-moved).at[receiver].add(moved)
    items = jnp.searchsorted(jnp.cumsum(tallies), jnp.arange(rows * top), side="right").astype(jnp.int32)
    table = items.reshape(top, rows).T
    table = table[jax.random.permutation(jax.random.fold_in(own, 1), rows)]
    rotation = jax.random.randint(jax.random.fold_in(own, 2), (rows, 1), 0, top)
    return jnp.take_along_axis(table, (jnp.arange(top)[None, :] + rotation) % top, axis=1)


def portions_of(amount, total, most, skew, full):
    portions = [(1 << 20) // math.isqrt(standing ** skew) + 1 for standing in range(1, amount + 1)]
    largest = most if full else min(most, max(-(-total // amount), total * portions[0] // sum(portions)))
    least = 1 if total - largest >= amount - 1 else 0
    holding, rest = [largest] + [least] * (amount - 1), total - largest - least * (amount - 1)
    while rest > 0:
        free = [i for i in range(1, amount) if holding[i] < largest] or [i for i in range(1, amount) if holding[i] < most]
        pool, remaining = sum([portions[i] for i in free]), rest
        for i in free:
            extra = min(most - holding[i], max(1, remaining * portions[i] // pool), rest)
            holding[i] = holding[i] + extra
            rest = rest - extra
    return np.array(holding)


def gaussian(key, shape, deviation, limit, cuts=(), kind=jnp.bfloat16):
    values = deviation * jax.random.normal(key, shape, jnp.float32)
    if cuts:
        values = values * shard_levels(key, shape, cuts, -0.22, 0.18)
    return jnp.clip(values, -limit, limit).astype(kind)


def setup_inputs(seed: int = 0) -> dict:
    streams_of = jax.random.split(jax.random.key(seed), 15)
    feats = gaussian(streams_of[0], (VERT, F), 1.0, 6.0, ((0, 32),))
    adj_vals = jnp.clip(jnp.exp(math.log(0.099609375) - 2.3038113 * jax.random.uniform(streams_of[1], (VERT // TILE, TPR, TILE, TILE), jnp.float32) ** shard_levels(streams_of[1], (VERT // TILE, TPR, TILE, TILE), ((0, 32),), -0.2, 0.2)), 0.0099487305, 0.099609375).astype(jnp.bfloat16)
    adj_cols = set_ends(jax.random.randint(streams_of[2], (VERT // TILE, TPR), 0, ROWBLK), jax.random.fold_in(streams_of[2], 1), 0, ROWBLK - 1).astype(jnp.int32)
    hub_feats = gaussian(streams_of[3], (HUBS, F), 1.0, 6.0, ((0, 32),))
    hub_mirrors_keys = jax.random.split(jax.random.fold_in(streams_of[4], 1), HUBS // HUB_DEV)
    hub_mirrors_turns = jax.random.permutation(jax.random.fold_in(streams_of[4], 3), HUBS // HUB_DEV)
    hub_mirrors = jax.vmap(lambda own, number: shared_out(jax.random.fold_in(streams_of[4], 2), own, number, HUB_DEV, N_DOM, MIRRORS, CAP, 2))(hub_mirrors_keys, hub_mirrors_turns).reshape((HUBS, MIRRORS))
    hub_links = set_ends(jax.random.randint(streams_of[5], (HUBS, MIRRORS, LINKS), 0, V_DEV), jax.random.fold_in(streams_of[5], 1), 0, V_DEV - 1).astype(jnp.int32)
    labels = set_ends(jax.random.randint(streams_of[6], (VERT,), 0, C), jax.random.fold_in(streams_of[6], 1), 0, C - 1).astype(jnp.int32)
    groups = set_ends(ranked(streams_of[7], (VERT,), GROUPS, 2), jax.random.fold_in(streams_of[7], 3), 0, GROUPS - 1).astype(jnp.int32)
    train_mask = set_ends((jax.random.randint(streams_of[8], (VERT,), 0, 2) < 1).astype(jnp.int32), jax.random.fold_in(streams_of[8], 1), 0, 1)
    w_self = gaussian(streams_of[9], (F, H), F ** -0.5, 0.5)
    w_neigh = gaussian(streams_of[10], (F, H), F ** -0.5, 0.5)
    bias = gaussian(streams_of[11], (H,), 0.5, 3.0, (), jnp.float32)
    w_cls = draw_w_cls(jax.random.fold_in(streams_of[14], 71), 0)
    group_logw = draw_group_logw(jax.random.fold_in(streams_of[14], 71), 0)
    return dict(feats=feats, adj_vals=adj_vals, adj_cols=adj_cols, hub_feats=hub_feats, hub_mirrors=hub_mirrors, hub_links=hub_links, labels=labels, groups=groups, train_mask=train_mask, w_self=w_self, w_neigh=w_neigh, bias=bias, w_cls=w_cls, group_logw=group_logw)


drift_rate = 0.5


def spread_links(source_rows, targets, dump_row):
    totals = jnp.zeros((dump_row + 1, source_rows.shape[1]), jnp.float32)
    counted = jnp.zeros((dump_row + 1,), jnp.float32)
    unit_rows = jnp.ones((targets.shape[0],), jnp.float32)
    for link_index in range(targets.shape[1]):
        totals = totals + jax.ops.segment_sum(source_rows, targets[:, link_index], num_segments=dump_row + 1)
        counted = counted + jax.ops.segment_sum(unit_rows, targets[:, link_index], num_segments=dump_row + 1)
    return totals[:dump_row], counted[:dump_row]


def gather_links(values, targets):
    padded = jnp.concatenate([values, jnp.zeros((1, values.shape[1]), jnp.float32)], axis=0)
    totals = jnp.zeros((targets.shape[0], values.shape[1]), jnp.float32)
    for link_index in range(targets.shape[1]):
        totals = totals + padded[targets[:, link_index]]
    return totals


def hub_targets(hub_mirrors, hub_links, device, dump_row):
    matched = hub_mirrors == device
    chosen = jnp.sum(jnp.where(matched[:, :, None], hub_links, 0), axis=1)
    present = jnp.any(matched, axis=1)
    return jnp.where(present[:, None], chosen, dump_row).astype(jnp.int32)


def local_sums(feats_part, vals_part, cols_part):
    row_blocks = cols_part.shape[0]
    tile_side = vals_part.shape[2]
    blocks = feats_part.reshape(row_blocks, tile_side, -1)
    picked = blocks[cols_part]
    summed = jnp.einsum("rkij,rkjf->rif", vals_part.astype(jnp.float32), picked.astype(jnp.float32), precision=lax.Precision.HIGHEST)
    weight_mass = jnp.sum(vals_part.astype(jnp.float32), axis=(1, 3))
    return summed.reshape(row_blocks * tile_side, -1), weight_mass.reshape(-1)


def reference(feats, adj_vals, adj_cols, hub_feats, hub_mirrors, hub_links, labels, groups, train_mask, w_self, w_neigh, bias, w_cls, group_logw):
    hub_rows = hub_feats.astype(jnp.float32)
    group_ids = jnp.arange(GROUPS)
    class_ids = jnp.arange(C)

    def forward(device):
        start = (device * V_DEV).astype(jnp.int32)
        block_start = (device * ROWBLK).astype(jnp.int32)
        feats_part = lax.dynamic_slice_in_dim(feats, start, V_DEV, 0)
        vals_part = lax.dynamic_slice_in_dim(adj_vals, block_start, ROWBLK, 0)
        cols_part = lax.dynamic_slice_in_dim(adj_cols, block_start, ROWBLK, 0)
        label_part = lax.dynamic_slice_in_dim(labels, start, V_DEV, 0)
        group_part = lax.dynamic_slice_in_dim(groups, start, V_DEV, 0)
        mask_part = lax.dynamic_slice_in_dim(train_mask, start, V_DEV, 0).astype(jnp.float32)
        targets = hub_targets(hub_mirrors, hub_links, device, V_DEV)
        hub_sum, hub_hits = spread_links(hub_rows, targets, V_DEV)
        local, mass = local_sums(feats_part, vals_part, cols_part)
        denom = 1.0 + mass + hub_hits
        agg = ((feats_part.astype(jnp.float32) + local + hub_sum) / denom[:, None]).astype(jnp.bfloat16)
        pre = jnp.dot(feats_part, w_self, preferred_element_type=jnp.float32) + jnp.dot(agg, w_neigh, preferred_element_type=jnp.float32) + bias
        hidden = jnp.maximum(pre, 0.0).astype(jnp.bfloat16)
        logits = jnp.dot(hidden, w_cls, preferred_element_type=jnp.float32)
        label_hot = (label_part[:, None] == class_ids[None, :]).astype(jnp.float32)
        loss = (jax.nn.logsumexp(logits, axis=1) - jnp.sum(logits * label_hot, axis=1)) * mask_part
        group_hot = (group_part[:, None] == group_ids[None, :]).astype(jnp.float32)
        return dict(feats_part=feats_part, targets=targets, denom=denom, agg=agg, pre=pre, hidden=hidden, logits=logits, label_hot=label_hot, loss=loss, group_hot=group_hot, mask_part=mask_part)

    def first_pass(carry, device):
        state = forward(device)
        loss_sums = carry[0] + jnp.sum(state["loss"][:, None] * state["group_hot"], axis=0)
        count_sums = carry[1] + jnp.sum(state["mask_part"][:, None] * state["group_hot"], axis=0)
        return (loss_sums, count_sums), None

    zero_groups = jnp.zeros((GROUPS,), jnp.float32)
    (gsum, gcount), _ = lax.scan(first_pass, (zero_groups, zero_groups), jnp.arange(N_DOM, dtype=jnp.int32))
    weights = GROUPS * jax.nn.softmax(group_logw + drift_rate * gsum / (gcount + 1.0))
    objective = jnp.sum(weights * gsum)

    def second_pass(carry, device):
        state = forward(device)
        vertex_weight = state["mask_part"] * jnp.sum(state["group_hot"] * weights[None, :], axis=1)
        probs = jax.nn.softmax(state["logits"], axis=1)
        dlogits = (vertex_weight[:, None] * (probs - state["label_hot"])).astype(jnp.bfloat16)
        gwc = jnp.dot(state["hidden"].T, dlogits, preferred_element_type=jnp.float32)
        dhidden = jnp.dot(dlogits, w_cls.T, preferred_element_type=jnp.float32)
        dpre_full = jnp.where(state["pre"] > 0.0, dhidden, 0.0)
        gbias = jnp.sum(dpre_full, axis=0)
        dpre = dpre_full.astype(jnp.bfloat16)
        gws = jnp.dot(state["feats_part"].T, dpre, preferred_element_type=jnp.float32)
        gwn = jnp.dot(state["agg"].T, dpre, preferred_element_type=jnp.float32)
        dagg = jnp.dot(dpre, w_neigh.T, preferred_element_type=jnp.float32)
        dsum = dagg / state["denom"][:, None]
        hub_part = gather_links(dsum, state["targets"])
        return (carry[0] + gws, carry[1] + gwn, carry[2] + gbias, carry[3] + gwc, carry[4] + hub_part), None

    start_carry = (jnp.zeros((F, H), jnp.float32), jnp.zeros((F, H), jnp.float32), jnp.zeros((H,), jnp.float32), jnp.zeros((H, C), jnp.float32), jnp.zeros((HUBS, F), jnp.float32))
    (grad_w_self, grad_w_neigh, grad_bias, grad_w_cls, hub_grad), _ = lax.scan(second_pass, start_carry, jnp.arange(N_DOM, dtype=jnp.int32))
    return (objective, grad_w_self, grad_w_neigh, grad_bias, grad_w_cls, hub_grad)
```

```python
import functools

import jax
import jax.numpy as jnp
from jax import lax
from jax.experimental import pallas as pl
from jax.experimental.pallas import tpu as pltpu
from jax.sharding import PartitionSpec as P

drift_rate = 0.5
LANES = 128
F32 = jnp.float32
BF16 = jnp.bfloat16
I32 = jnp.int32


def dot_nn(a, b):
    return lax.dot_general(a, b, (((1,), (0,)), ((), ())), preferred_element_type=F32)


def dot_nt(a, b):
    return lax.dot_general(a, b, (((1,), (1,)), ((), ())), preferred_element_type=F32)


def dot_tn(a, b):
    return lax.dot_general(a, b, (((0,), (0,)), ((), ())), preferred_element_type=F32)


def iota(shape, dim):
    return lax.broadcasted_iota(I32, shape, dim)


def params(n_grid=0, mib=56):
    kw = {} if n_grid == 0 else {"dimension_semantics": ("arbitrary",) * n_grid}
    return pltpu.CompilerParams(vmem_limit_bytes=mib << 20, **kw)


def pack_kernel(n, cap, me_ref, hub_ref, mir_ref, link_ref, out_ref, place_ref):
    hubs, width = hub_ref.shape
    mirrors, links = link_ref.shape[0], link_ref.shape[1]
    dest = iota((n, hubs), 0)
    present = jnp.zeros((n, hubs), F32)
    for j in range(mirrors):
        present = present + jnp.where(mir_ref[j : j + 1, :] == dest, 1.0, 0.0)
    before = jnp.where(iota((hubs, hubs), 0) < iota((hubs, hubs), 1), 1.0, 0.0)
    rank = dot_nn(present.astype(BF16), before.astype(BF16))
    rank = jnp.where(present > 0.0, rank, 9999.0).astype(I32)
    place = jnp.where(rank[:, None, :] == iota((n, cap, hubs), 1), 1.0, 0.0)
    place = place.reshape(n * cap, hubs).astype(BF16)
    place_ref[...] = place
    rows = dot_nn(place, hub_ref[...])
    out_ref[:, 0:cap, :] = rows.reshape(n, cap, width).astype(BF16)
    dest3 = iota((n, links, hubs), 0)
    ends = jnp.zeros((n, links, hubs), I32)
    for j in range(mirrors):
        ends = ends + jnp.where(mir_ref[j : j + 1, :][None] == dest3, link_ref[j][None], 0)
    high = ((ends >> 7) + 1).astype(F32)
    low = (ends & 127).astype(F32)
    both = jnp.concatenate([high, low], axis=1).astype(BF16)
    offset = (me_ref[0] * cap) % LANES
    lane_of = rank[:, None, :] + offset == iota((n, LANES, hubs), 1)
    lane_of = jnp.where(lane_of, 1.0, 0.0).astype(BF16)
    packed = lax.dot_general(
        both, lane_of, (((2,), (2,)), ((0,), (0,))), preferred_element_type=F32
    )
    out_ref[:, cap : cap + 2 * links, :] = packed.astype(BF16)


def local_kernel(tiles, cols_ref, feats_ref, vals_ref, s_ref, ft_ref, mass_ref, turned):
    step = pl.program_id(0)
    width = feats_ref.shape[1]
    blocks = turned.shape[0]

    @pl.when(step == 0)
    def _():
        def turn(b, carry):
            rows = feats_ref[pl.ds(pl.multiple_of(b * LANES, LANES), LANES), :]
            turned[b, 0:width, :] = rows.astype(F32).T.astype(BF16)
            turned[b, width:, :] = jnp.ones((16, LANES), BF16)
            return carry

        lax.fori_loop(0, blocks, turn, 0, unroll=4)

    per_step = vals_ref.shape[0]
    for r in range(per_step):
        block = step * per_step + r
        left = jnp.concatenate([turned[cols_ref[block, k]] for k in range(tiles)], axis=1)
        right = jnp.concatenate([vals_ref[r, k] for k in range(tiles)], axis=1)
        both = dot_nt(left, right)
        own = turned[block, 0:width, :]
        span = slice(r * LANES, (r + 1) * LANES)
        s_ref[:, span] = own.astype(F32) + both[0:width]
        ft_ref[:, span] = own
        mass_ref[:, span] = both[width : width + 8]


def lane_row(ref, step, parts):
    return jnp.concatenate([ref[pl.ds(step * parts + k, 1), :] for k in range(parts)], axis=1)


def fold_lanes(x):
    total = x[:, 0:LANES]
    for k in range(1, x.shape[1] // LANES):
        total = total + x[:, k * LANES : (k + 1) * LANES]
    return total


def forward_kernel(
    n, cap, links, classes, span,
    recv_ref, s_ref, ft_ref, mass_ref, label_ref, group_ref, mask_ref, w_ref, bias_ref, wc_ref,
    fa_ref, hid_ref, pmo_ref, m_ref, inv_ref, sums_ref,
    src, word_of, value_of, loss_acc, count_acc,
):
    step = pl.program_id(0)
    slots = n * cap
    width = s_ref.shape[0]
    groups = loss_acc.shape[0]
    parts = span // LANES

    @pl.when(step == 0)
    def _():
        loss_acc[...] = jnp.zeros_like(loss_acc)
        count_acc[...] = jnp.zeros_like(count_acc)
        per = LANES // cap
        for b in range(slots // LANES):
            rows = recv_ref[b * per : (b + 1) * per, 0:cap, :].astype(F32).reshape(LANES, width)
            src[0:width, b * LANES : (b + 1) * LANES] = rows.T.astype(BF16)
            ends = recv_ref[b * per, cap : cap + 2 * links, :].astype(F32)
            for k in range(1, per):
                ends = ends + recv_ref[b * per + k, cap : cap + 2 * links, :].astype(F32)
            target = ((ends[0:links] - 1.0) * 128.0 + ends[links:]).astype(I32)
            word_of[:, b * LANES : (b + 1) * LANES] = target >> 3
            value_of[:, b * LANES : (b + 1) * LANES] = jnp.left_shift(1, (target & 7) * 4)
        src[width:, :] = jnp.ones((16, slots), BF16)

    chunk = 256
    for b in range(parts):
        first = (step * span + b * LANES) // 8
        for c in range(slots // chunk):
            at = slice(c * chunk, (c + 1) * chunk)
            rows16 = iota((16, chunk), 0) + first
            words = jnp.zeros((16, chunk), I32)
            for k in range(links):
                words = words + jnp.where(
                    word_of[k : k + 1, at] == rows16, value_of[k : k + 1, at], 0
                )
            wide = jnp.broadcast_to(words[:, None, :], (16, 8, chunk))
            count = (wide >> (4 * iota((16, 8, chunk), 1))) & 15
            m_ref[b * LANES : (b + 1) * LANES, at] = (
                count.reshape(LANES, chunk).astype(F32).astype(BF16)
            )
    hub = dot_nt(src[...], m_ref[...])
    denom = 1.0 + mass_ref[0:1, :] + hub[width : width + 1, :]
    inverse = 1.0 / denom
    inv_ref[...] = jnp.broadcast_to(inverse, inv_ref.shape)
    agg = ((s_ref[...] + hub[0:width]) * inverse).astype(BF16)
    fa_ref[0:width, :] = ft_ref[...]
    fa_ref[width:, :] = agg
    pre = dot_nn(w_ref[...], fa_ref[...]) + bias_ref[:, 0:1]
    hidden = jnp.maximum(pre, 0.0).astype(BF16)
    hid_ref[...] = hidden
    logits = dot_nn(wc_ref[...], hidden)
    class_row = iota(logits.shape, 0)
    logits = jnp.where(class_row < classes, logits, -jnp.inf)
    top = jnp.max(logits, axis=0, keepdims=True)
    shifted = jnp.exp(logits - top)
    total = jnp.sum(shifted, axis=0, keepdims=True)
    mask = lane_row(mask_ref, step, parts).astype(F32)
    hot = class_row == lane_row(label_ref, step, parts)
    picked = jnp.sum(jnp.where(hot, logits, 0.0), axis=0, keepdims=True)
    loss = (top + jnp.log(total) - picked) * mask
    pmo_ref[...] = mask * (shifted * (1.0 / total) - jnp.where(hot, 1.0, 0.0))
    in_group = iota((groups, span), 0) == lane_row(group_ref, step, parts)
    loss_acc[...] += fold_lanes(jnp.where(in_group, loss, 0.0))
    count_acc[...] += fold_lanes(jnp.where(in_group, mask, 0.0))

    @pl.when(step == pl.num_programs(0) - 1)
    def _():
        sub, lane = iota((groups, LANES), 0), iota((groups, LANES), 1)
        loss_col = jnp.sum(loss_acc[...], axis=1, keepdims=True)
        count_col = jnp.sum(count_acc[...], axis=1, keepdims=True)
        both = jnp.where(lane == sub, loss_col, 0.0) + jnp.where(
            lane == sub + groups, count_col, 0.0
        )
        row = jnp.sum(both, axis=0, keepdims=True)
        sums_ref[...] = jnp.broadcast_to(row[None], sums_ref.shape)


def backward_kernel(
    n, cap, share, span,
    sums_ref, logw_ref, pmo_ref, hid_ref, fa_ref, m_ref, inv_ref, group_ref, wc_ref, wn_ref,
    msg_ref, obj_ref,
    q_col, gw, gwc, gb, slot, flat,
):
    step = pl.program_id(0)
    groups = logw_ref.shape[1]
    slots = n * cap
    parts = span // LANES
    hidden_rows = gb.shape[0]
    both_rows = fa_ref.shape[0]
    class_rows = pmo_ref.shape[0]

    @pl.when(step == 0)
    def _():
        row = jnp.sum(sums_ref[...], axis=0)
        sub, lane = iota((groups, LANES), 0), iota((groups, LANES), 1)
        gsum = jnp.sum(jnp.where(lane == sub, row, 0.0), axis=1, keepdims=True)
        gcount = jnp.sum(jnp.where(lane == sub + groups, row, 0.0), axis=1, keepdims=True)
        sub, lane = iota((groups, groups), 0), iota((groups, groups), 1)
        logw = jnp.sum(jnp.where(lane == sub, logw_ref[...], 0.0), axis=1, keepdims=True)
        score = logw + drift_rate * gsum / (gcount + 1.0)
        e = jnp.exp(score - jnp.max(score, axis=0, keepdims=True))
        q = groups * (e / jnp.sum(e, axis=0, keepdims=True))
        obj_ref[0, 0] = jnp.sum(q * gsum)
        q_col[...] = jnp.broadcast_to(q, q_col.shape)
        gw[...] = jnp.zeros_like(gw)
        gwc[...] = jnp.zeros_like(gwc)
        gb[...] = jnp.zeros_like(gb)
        slot[...] = jnp.zeros_like(slot)

    in_group = iota((groups, span), 0) == lane_row(group_ref, step, parts)
    weight = jnp.sum(jnp.where(in_group, q_col[:, 0:1], 0.0), axis=0, keepdims=True)
    dlogits = (pmo_ref[...] * weight).astype(BF16)
    hidden = hid_ref[...]
    gwc[...] += dot_nt(dlogits, hidden)
    dhidden = dot_nn(wc_ref[...], dlogits)
    dfull = jnp.where(hidden.astype(F32) > 0.0, dhidden, 0.0)
    gb[...] += fold_lanes(dfull)
    dpre = dfull.astype(BF16)
    gw[...] += dot_nt(fa_ref[...], dpre)
    dagg = dot_nn(wn_ref[...], dpre)
    dsum = (dagg * inv_ref[0:1, :]).astype(BF16)
    slot[...] += dot_nn(dsum, m_ref[...])

    @pl.when(step == pl.num_programs(0) - 1)
    def _():
        per = LANES // cap
        for b in range(slots // LANES):
            rows = slot[:, b * LANES : (b + 1) * LANES].T
            msg_ref[b * per : (b + 1) * per, 0:cap, :] = rows.reshape(per, cap, LANES).astype(BF16)
        row = 0
        for b in range(hidden_rows // LANES):
            flat[row : row + both_rows, :] = gw[:, b * LANES : (b + 1) * LANES]
            row += both_rows
        for b in range(hidden_rows // LANES):
            flat[row : row + class_rows, :] = gwc[:, b * LANES : (b + 1) * LANES]
            row += class_rows
        flat[row:, :] = jnp.zeros((flat.shape[0] - row, LANES), F32)
        sub, lane = iota((LANES, LANES), 0), iota((LANES, LANES), 1)
        for b in range(hidden_rows // LANES):
            col = jnp.sum(gb[b * LANES : (b + 1) * LANES, :], axis=1, keepdims=True)
            flat[row + b : row + b + 1, :] = jnp.sum(
                jnp.where(sub == lane, col, 0.0), axis=0, keepdims=True
            )
        for d in range(n):
            msg_ref[d, cap : cap + share, :] = flat[d * share : (d + 1) * share, :].astype(BF16)


def reduce_kernel(cap, share, recv_ref, out_ref):
    total = recv_ref[0, cap : cap + share, :].astype(F32)
    for d in range(1, recv_ref.shape[0]):
        total = total + recv_ref[d, cap : cap + share, :].astype(F32)
    out_ref[...] = jnp.broadcast_to(total.astype(BF16)[None], out_ref.shape)


def hub_kernel(cap, recv_ref, place_ref, out_ref):
    n, width = recv_ref.shape[0], recv_ref.shape[2]
    rows = recv_ref[:, 0:cap, :].astype(F32).reshape(n * cap, width).astype(BF16)
    out_ref[...] = dot_tn(place_ref[...], rows)


def unpack_kernel(recv_ref, gws_ref, gwn_ref, gb_ref, gwc_ref, flat):
    n, share = recv_ref.shape[0], recv_ref.shape[1]
    for d in range(n):
        flat[d * share : (d + 1) * share, :] = recv_ref[d].astype(F32)
    width, hidden_rows = gws_ref.shape
    classes = gwc_ref.shape[1]
    class_rows = -(-classes // 16) * 16
    row = 0
    for b in range(hidden_rows // LANES):
        at = slice(b * LANES, (b + 1) * LANES)
        gws_ref[:, at] = flat[row : row + width, :]
        gwn_ref[:, at] = flat[row + width : row + 2 * width, :]
        row += 2 * width
    for b in range(hidden_rows // LANES):
        turned = flat[row : row + class_rows, :].T
        gwc_ref[b * LANES : (b + 1) * LANES, :] = turned[:, 0:classes]
        row += class_rows
    gb_ref[...] = flat[row : row + hidden_rows // LANES, :]


def exchange(x):
    return lax.all_to_all(x, "dom", split_axis=0, concat_axis=0, tiled=True)


def on_device(
    feats, adj_vals, adj_cols, hub_feats, hub_mirrors, hub_links, labels, groups, train_mask,
    w_self, w_neigh, bias, w_cls, group_logw,
):
    verts, width = feats.shape
    n = lax.axis_size("dom")
    hub_dev = hub_feats.shape[0]
    mirrors = hub_mirrors.shape[1]
    links = hub_links.shape[2]
    group_total = group_logw.shape[0]
    hidden_rows, classes = w_cls.shape
    class_rows = -(-classes // 16) * 16
    row_blocks, tiles = adj_cols.shape
    cap = min(hub_dev, max(2, 2 * hub_dev * mirrors // n))
    slots = n * cap
    any_space = pl.BlockSpec(memory_space=pltpu.VMEM)
    smem = pl.BlockSpec(memory_space=pltpu.SMEM)
    sds = jax.ShapeDtypeStruct

    me = lax.axis_index("dom").reshape(1).astype(I32)
    packed, place = pl.pallas_call(
        functools.partial(pack_kernel, n, cap),
        name="pack",
        out_shape=(sds((n, cap + 2 * links, width), BF16), sds((slots, hub_dev), BF16)),
        in_specs=[smem, any_space, any_space, any_space],
        out_specs=(any_space, any_space),
        compiler_params=params(),
    )(me, hub_feats, hub_mirrors.T, hub_links.transpose(1, 2, 0))
    recv = exchange(packed)

    per_step = 4
    span = per_step * LANES
    steps = row_blocks // per_step
    cols_at = lambda i, *_: (0, i)
    s_turned, f_turned, mass = pl.pallas_call(
        functools.partial(local_kernel, tiles),
        name="local",
        grid_spec=pltpu.PrefetchScalarGridSpec(
            num_scalar_prefetch=1,
            grid=(steps,),
            in_specs=[
                pl.BlockSpec((verts, width), lambda i, *_: (0, 0)),
                pl.BlockSpec((per_step, tiles, LANES, LANES), lambda i, *_: (i, 0, 0, 0)),
            ],
            out_specs=[
                pl.BlockSpec((width, span), cols_at),
                pl.BlockSpec((width, span), cols_at),
                pl.BlockSpec((8, span), cols_at),
            ],
            scratch_shapes=[pltpu.VMEM((row_blocks, width + 16, LANES), BF16)],
        ),
        out_shape=(sds((width, verts), F32), sds((width, verts), BF16), sds((8, verts), F32)),
        compiler_params=params(1),
    )(adj_cols, feats, adj_vals)

    table = (verts // LANES, LANES)
    label_table, group_table = labels.reshape(table), groups.reshape(table)
    mask_table = train_mask.reshape(table)
    w_turned = jnp.concatenate([w_self, w_neigh], axis=0).T
    wc_padded = jnp.pad(w_cls, ((0, 0), (0, class_rows - classes)))
    whole = lambda *shape: pl.BlockSpec(shape, lambda i: (0,) * len(shape))
    fa, hid, pmo, counts, inv, sums = pl.pallas_call(
        functools.partial(forward_kernel, n, cap, links, classes, span),
        name="forward",
        grid=(steps,),
        in_specs=[
            whole(n, cap + 2 * links, width),
            pl.BlockSpec((width, span), cols_at),
            pl.BlockSpec((width, span), cols_at),
            pl.BlockSpec((8, span), cols_at),
            whole(*table),
            whole(*table),
            whole(*table),
            whole(hidden_rows, 2 * width),
            whole(hidden_rows, 1),
            whole(class_rows, hidden_rows),
        ],
        out_specs=[
            pl.BlockSpec((2 * width, span), cols_at),
            pl.BlockSpec((hidden_rows, span), cols_at),
            pl.BlockSpec((class_rows, span), cols_at),
            pl.BlockSpec((span, slots), lambda i: (i, 0)),
            pl.BlockSpec((8, span), cols_at),
            whole(n, 1, LANES),
        ],
        out_shape=(
            sds((2 * width, verts), BF16),
            sds((hidden_rows, verts), BF16),
            sds((class_rows, verts), F32),
            sds((verts, slots), BF16),
            sds((8, verts), F32),
            sds((n, 1, LANES), F32),
        ),
        scratch_shapes=[
            pltpu.VMEM((width + 16, slots), BF16),
            pltpu.VMEM((links, slots), I32),
            pltpu.VMEM((links, slots), I32),
            pltpu.VMEM((group_total, LANES), F32),
            pltpu.VMEM((group_total, LANES), F32),
        ],
        compiler_params=params(1),
    )(
        recv, s_turned, f_turned, mass, label_table, group_table, mask_table,
        w_turned, bias.reshape(hidden_rows, 1), wc_padded.T,
    )
    all_sums = exchange(sums)

    grad_rows = hidden_rows // LANES * (2 * width + class_rows + 1)
    share = -(-grad_rows // (8 * n)) * 8
    message, objective = pl.pallas_call(
        functools.partial(backward_kernel, n, cap, share, span),
        name="backward",
        grid=(steps,),
        in_specs=[
            whole(n, 1, LANES),
            whole(1, group_total),
            pl.BlockSpec((class_rows, span), cols_at),
            pl.BlockSpec((hidden_rows, span), cols_at),
            pl.BlockSpec((2 * width, span), cols_at),
            pl.BlockSpec((span, slots), lambda i: (i, 0)),
            pl.BlockSpec((8, span), cols_at),
            whole(*table),
            whole(hidden_rows, class_rows),
            whole(width, hidden_rows),
        ],
        out_specs=[whole(n, cap + share, LANES), smem],
        out_shape=(sds((n, cap + share, LANES), BF16), sds((1, 1), F32)),
        scratch_shapes=[
            pltpu.VMEM((group_total, LANES), F32),
            pltpu.VMEM((2 * width, hidden_rows), F32),
            pltpu.VMEM((class_rows, hidden_rows), F32),
            pltpu.VMEM((hidden_rows, LANES), F32),
            pltpu.VMEM((width, slots), F32),
            pltpu.VMEM((n * share, LANES), F32),
        ],
        compiler_params=params(1),
    )(
        all_sums, group_logw.reshape(1, group_total), pmo, hid, fa, counts, inv, group_table,
        wc_padded, w_neigh,
    )
    answer = exchange(message)

    reduced = pl.pallas_call(
        functools.partial(reduce_kernel, cap, share),
        name="reduce",
        out_shape=sds((n, share, LANES), BF16),
        in_specs=[any_space],
        out_specs=any_space,
        compiler_params=params(),
    )(answer)
    gathered = exchange(reduced)
    hub_grad = pl.pallas_call(
        functools.partial(hub_kernel, cap),
        name="hubgrad",
        out_shape=sds((hub_dev, width), F32),
        in_specs=[any_space, any_space],
        out_specs=any_space,
        compiler_params=params(),
    )(answer, place)
    grad_w_self, grad_w_neigh, grad_bias, grad_w_cls = pl.pallas_call(
        unpack_kernel,
        name="unpack",
        out_shape=(
            sds((width, hidden_rows), F32),
            sds((width, hidden_rows), F32),
            sds((hidden_rows // LANES, LANES), F32),
            sds((hidden_rows, classes), F32),
        ),
        in_specs=[any_space],
        out_specs=(any_space,) * 4,
        scratch_shapes=[pltpu.VMEM((n * share, LANES), F32)],
        compiler_params=params(),
    )(gathered)
    return (
        objective.reshape(()), grad_w_self, grad_w_neigh, grad_bias.reshape(hidden_rows),
        grad_w_cls, hub_grad,
    )


def solution(mesh):
    in_specs = (
        P("dom", None),
        P("dom", None, None, None),
        P("dom", None),
        P("dom", None),
        P("dom", None),
        P("dom", None, None),
        P("dom"),
        P("dom"),
        P("dom"),
        P(),
        P(),
        P(),
        P(),
        P(),
    )
    out_specs = (P(), P(), P(), P(), P(), P("dom", None))
    return jax.shard_map(
        on_device, mesh=mesh, in_specs=in_specs, out_specs=out_specs, check_vma=False
    )
```

```python
import functools

import jax
import jax.numpy as jnp
from jax import lax
from jax.experimental import pallas as pl
from jax.experimental.pallas import tpu as pltpu
from jax.sharding import PartitionSpec as P

drift_rate = 0.5
LANES = 128
F32 = jnp.float32
BF16 = jnp.bfloat16
I32 = jnp.int32


def dot_nn(a, b):
    return lax.dot_general(a, b, (((1,), (0,)), ((), ())), preferred_element_type=F32)


def dot_nt(a, b):
    return lax.dot_general(a, b, (((1,), (1,)), ((), ())), preferred_element_type=F32)


def dot_tn(a, b):
    return lax.dot_general(a, b, (((0,), (0,)), ((), ())), preferred_element_type=F32)


def iota(shape, dim):
    return lax.broadcasted_iota(I32, shape, dim)


on_chip = pltpu.VMEM


def keep(x):
    return pltpu.with_memory_space_constraint(x, pltpu.VMEM)


def off_chip(x):
    return pltpu.with_memory_space_constraint(x, pltpu.HBM)


def params(n_grid=0, mib=20):
    kw = {} if n_grid == 0 else {"dimension_semantics": ("arbitrary",) * n_grid}
    return pltpu.CompilerParams(vmem_limit_bytes=mib << 20, **kw)


def pack_kernel(n, cap, me_ref, hub_ref, mir_ref, link_ref, out_ref, place_ref):
    hubs, width = hub_ref.shape
    mirrors, links = link_ref.shape[0], link_ref.shape[1]
    dest = iota((n, hubs), 0)
    present = jnp.zeros((n, hubs), F32)
    for j in range(mirrors):
        present = present + jnp.where(mir_ref[j : j + 1, :] == dest, 1.0, 0.0)
    before = jnp.where(iota((hubs, hubs), 0) < iota((hubs, hubs), 1), 1.0, 0.0)
    rank = dot_nn(present.astype(BF16), before.astype(BF16))
    rank = jnp.where(present > 0.0, rank, 9999.0).astype(I32)
    place = jnp.where(rank[:, None, :] == iota((n, cap, hubs), 1), 1.0, 0.0)
    place = place.reshape(n * cap, hubs).astype(BF16)
    place_ref[...] = place
    rows = dot_nn(place, hub_ref[...])
    out_ref[:, 0:cap, :] = rows.reshape(n, cap, width).astype(BF16)
    dest3 = iota((n, links, hubs), 0)
    ends = jnp.zeros((n, links, hubs), I32)
    for j in range(mirrors):
        ends = ends + jnp.where(mir_ref[j : j + 1, :][None] == dest3, link_ref[j][None], 0)
    high = ((ends >> 7) + 1).astype(F32)
    low = (ends & 127).astype(F32)
    both = jnp.concatenate([high, low], axis=1).astype(BF16)
    offset = (me_ref[0] * cap) % LANES
    lane_of = rank[:, None, :] + offset == iota((n, LANES, hubs), 1)
    lane_of = jnp.where(lane_of, 1.0, 0.0).astype(BF16)
    packed = lax.dot_general(
        both, lane_of, (((2,), (2,)), ((0,), (0,))), preferred_element_type=F32
    )
    out_ref[:, cap : cap + 2 * links, :] = packed.astype(BF16)


def to_row(block):
    eye = iota(block.shape, 0) == iota(block.shape, 1)
    return jnp.sum(jnp.where(eye, block, 0.0), axis=0, keepdims=True)


def to_column(row):
    eye = iota((LANES, LANES), 0) == iota((LANES, LANES), 1)
    return jnp.sum(jnp.where(eye, row, 0.0), axis=1, keepdims=True)


def turn(x):
    return x.astype(F32).T


def local_kernel(
    tiles, cols_ref, feats_ref, vals_ref, ws_ref, wn_ref, wc_ref, bias_ref,
    s_ref, ft_ref, mass_ref, w_ref, wct_ref, wcn_ref, biasb_ref, wide,
):
    step = pl.program_id(0)
    width = feats_ref.shape[1]
    blocks = wide.shape[0]
    hidden_rows = ws_ref.shape[1]
    classes = wc_ref.shape[0]
    class_rows = wct_ref.shape[0]

    @pl.when(step == 0)
    def _():
        def fill(b, carry):
            wide[b, :, 0:width] = feats_ref[pl.ds(pl.multiple_of(b * LANES, LANES), LANES), :]
            wide[b, :, width:] = jnp.ones((LANES, LANES), BF16)
            return carry

        lax.fori_loop(0, blocks, fill, 0, unroll=4)
        wct_ref[...] = jnp.zeros_like(wct_ref)
        wct_ref[0:classes, :] = wc_ref[...]
        for b in range(hidden_rows // LANES):
            at = slice(b * LANES, (b + 1) * LANES)
            w_ref[at, 0:width] = turn(ws_ref[:, at]).astype(BF16)
            w_ref[at, width:] = turn(wn_ref[:, at]).astype(BF16)
            wcn_ref[at, :] = turn(wct_ref[:, at]).astype(BF16)
            biasb_ref[at, :] = jnp.broadcast_to(to_column(bias_ref[b : b + 1, :]), (LANES, LANES))

    per_step = vals_ref.shape[0]
    parts = s_ref.shape[1] // LANES
    for r in range(per_step):
        block = step * per_step + r
        home, part = step * (per_step // parts) + r // parts, r % parts
        span = slice(part * LANES, (part + 1) * LANES)
        left = jnp.concatenate([vals_ref[r, k] for k in range(tiles)], axis=1)
        right = jnp.concatenate([wide[cols_ref[k, block]] for k in range(tiles)], axis=0)
        both = dot_nn(left, right)
        own = wide[block, :, 0:width].astype(F32)
        s_ref[r // parts, span, :] = own + both[:, 0:width]
        ft_ref[home, :, span] = own.T.astype(BF16)
        mass_ref[home, :, span] = to_row(both[:, width : width + LANES])


def lane_row(ref, step, parts):
    return jnp.concatenate([ref[pl.ds(step * parts + k, 1), :] for k in range(parts)], axis=1)


def fold_lanes(x):
    total = x[:, 0:LANES]
    for k in range(1, x.shape[1] // LANES):
        total = total + x[:, k * LANES : (k + 1) * LANES]
    return total


def forward_kernel(
    n, cap, links, classes, span,
    recv_ref, s_ref, ft_ref, mass_ref, label_ref, group_ref, mask_ref, w_ref, bias_ref, wc_ref,
    agg_ref, hid_ref, pmo_ref, m_ref, inv_ref, of_ref, sums_ref,
    src, word_of, value_of, loss_acc, count_acc,
):
    step = pl.program_id(0)
    slots = n * cap
    width = s_ref.shape[2]
    groups = loss_acc.shape[0]
    parts = span // LANES

    @pl.when(step == 0)
    def _():
        loss_acc[...] = jnp.zeros_like(loss_acc)
        count_acc[...] = jnp.zeros_like(count_acc)
        per = LANES // cap
        for b in range(slots // LANES):
            at = slice(b * LANES, (b + 1) * LANES)
            rows = recv_ref[b * per : (b + 1) * per, 0:cap, :].astype(F32).reshape(LANES, width)
            src[at, 0:width] = rows.astype(BF16)
            ends = recv_ref[b * per, cap : cap + 2 * links, :].astype(F32)
            for k in range(1, per):
                ends = ends + recv_ref[b * per + k, cap : cap + 2 * links, :].astype(F32)
            target = ((ends[0:links] - 1.0) * 128.0 + ends[links:]).astype(I32)
            word_of[:, at] = target >> 3
            value_of[:, at] = jnp.left_shift(1, (target & 7) * 4)
        src[:, width:] = jnp.ones((slots, LANES), BF16)

    chunk = 256
    for b in range(parts):
        first = (step * span + b * LANES) // 8
        for c in range(slots // chunk):
            at = slice(c * chunk, (c + 1) * chunk)
            rows16 = iota((16, chunk), 0) + first
            words = jnp.zeros((16, chunk), I32)
            for k in range(links):
                words = words + jnp.where(
                    word_of[k : k + 1, at] == rows16, value_of[k : k + 1, at], 0
                )
            wide = jnp.broadcast_to(words[:, None, :], (16, 8, chunk))
            count = (wide >> (4 * iota((16, 8, chunk), 1))) & 15
            m_ref[0, b * LANES : (b + 1) * LANES, at] = (
                count.reshape(LANES, chunk).astype(F32).astype(BF16)
            )
    hub = dot_nn(m_ref[0], src[...])
    total = s_ref[0] + hub[:, 0:width]
    for b in range(parts):
        at = slice(b * LANES, (b + 1) * LANES)
        inverse = 1.0 / (1.0 + mass_ref[step, :, at] + to_row(hub[at, width : width + LANES]))
        inv_ref[step, :, at] = inverse
        agg_ref[step, :, at] = (total[at, :].T * inverse).astype(BF16)
    bias = jnp.concatenate([bias_ref[...]] * parts, axis=1)
    both = jnp.concatenate([ft_ref[step], agg_ref[step]], axis=0)
    pre = dot_nn(w_ref[...], both) + bias
    hidden = jnp.maximum(pre, 0.0).astype(BF16)
    hid_ref[step] = hidden
    logits = dot_nn(wc_ref[...], hidden)
    class_row = iota(logits.shape, 0)
    logits = jnp.where(class_row < classes, logits, -jnp.inf)
    top = jnp.max(logits, axis=0, keepdims=True)
    shifted = jnp.exp(logits - top)
    total = jnp.sum(shifted, axis=0, keepdims=True)
    mask = lane_row(mask_ref, step, parts).astype(F32)
    hot = class_row == lane_row(label_ref, step, parts)
    picked = jnp.sum(jnp.where(hot, logits, 0.0), axis=0, keepdims=True)
    loss = (top + jnp.log(total) - picked) * mask
    pmo_ref[step] = mask * (shifted * (1.0 / total) - jnp.where(hot, 1.0, 0.0))
    group_row = lane_row(group_ref, step, parts)
    of_ref[step] = group_row
    in_group = iota((groups, span), 0) == group_row
    loss_acc[...] += fold_lanes(jnp.where(in_group, loss, 0.0))
    count_acc[...] += fold_lanes(jnp.where(in_group, mask, 0.0))

    @pl.when(step == pl.num_programs(0) - 1)
    def _():
        sub, lane = iota((groups, LANES), 0), iota((groups, LANES), 1)
        loss_col = jnp.sum(loss_acc[...], axis=1, keepdims=True)
        count_col = jnp.sum(count_acc[...], axis=1, keepdims=True)
        both = jnp.where(lane == sub, loss_col, 0.0) + jnp.where(
            lane == sub + groups, count_col, 0.0
        )
        row = jnp.sum(both, axis=0, keepdims=True)
        sums_ref[...] = jnp.broadcast_to(row[None], sums_ref.shape)


def backward_kernel(
    span,
    sums_ref, logw_ref, pmo_ref, hid_ref, ft_ref, agg_ref, inv_ref, group_ref, wc_ref, wn_ref,
    msg_ref, obj_ref, dsum_ref,
    q_col, gw, gwc, gb, flat,
):
    step = pl.program_id(0)
    n, share = msg_ref.shape[0], msg_ref.shape[1]
    groups = logw_ref.shape[1]
    hidden_rows = gb.shape[0]
    class_rows = pmo_ref.shape[1]

    @pl.when(step == 0)
    def _():
        row = jnp.sum(sums_ref[...], axis=0)
        sub, lane = iota((groups, LANES), 0), iota((groups, LANES), 1)
        gsum = jnp.sum(jnp.where(lane == sub, row, 0.0), axis=1, keepdims=True)
        gcount = jnp.sum(jnp.where(lane == sub + groups, row, 0.0), axis=1, keepdims=True)
        sub, lane = iota((groups, groups), 0), iota((groups, groups), 1)
        logw = jnp.sum(jnp.where(lane == sub, logw_ref[...], 0.0), axis=1, keepdims=True)
        score = logw + drift_rate * gsum / (gcount + 1.0)
        e = jnp.exp(score - jnp.max(score, axis=0, keepdims=True))
        q = groups * (e / jnp.sum(e, axis=0, keepdims=True))
        obj_ref[0, 0] = jnp.sum(q * gsum)
        q_col[...] = jnp.broadcast_to(q, q_col.shape)
        gw[...] = jnp.zeros_like(gw)
        gwc[...] = jnp.zeros_like(gwc)
        gb[...] = jnp.zeros_like(gb)

    in_group = iota((groups, span), 0) == group_ref[step]
    weight = jnp.sum(jnp.where(in_group, q_col[:, 0:1], 0.0), axis=0, keepdims=True)
    dlogits = (pmo_ref[step] * weight).astype(BF16)
    hidden = hid_ref[step]
    gwc[...] += dot_nt(hidden, dlogits)
    dhidden = dot_nn(wc_ref[...], dlogits)
    dfull = jnp.where(hidden.astype(F32) > 0.0, dhidden, 0.0)
    gb[...] += fold_lanes(dfull)
    dpre = dfull.astype(BF16)
    gw[...] += dot_nt(dpre, jnp.concatenate([ft_ref[step], agg_ref[step]], axis=0))
    dagg = dot_nn(wn_ref[...], dpre)
    dsum_ref[step] = (dagg * inv_ref[step]).astype(BF16)

    @pl.when(step == pl.num_programs(0) - 1)
    def _():
        row = 0
        for b in range(gw.shape[1] // LANES):
            flat[row : row + hidden_rows, :] = gw[:, b * LANES : (b + 1) * LANES]
            row += hidden_rows
        for b in range(hidden_rows // LANES):
            flat[row : row + class_rows, :] = gwc[b * LANES : (b + 1) * LANES, :].T
            row += class_rows
        flat[row:, :] = jnp.zeros((flat.shape[0] - row, LANES), F32)
        for b in range(hidden_rows // LANES):
            col = jnp.sum(gb[b * LANES : (b + 1) * LANES, :], axis=1, keepdims=True)
            flat[row + b : row + b + 1, :] = to_row(jnp.broadcast_to(col, (LANES, LANES)))
        for d in range(n):
            msg_ref[d] = flat[d * share : (d + 1) * share, :].astype(BF16)


def slot_kernel(dsum_ref, m_ref, place_ref, out_ref, turned_ref, slot):
    step = pl.program_id(0)
    n, cap = out_ref.shape[0], out_ref.shape[1]
    slots = n * cap

    @pl.when(step == 0)
    def _():
        slot[...] = jnp.zeros_like(slot)
        for b in range(slots // LANES):
            at = slice(b * LANES, (b + 1) * LANES)
            turned_ref[:, at] = turn(place_ref[at, :]).astype(BF16)

    slot[...] += dot_nn(dsum_ref[step], m_ref[0])

    @pl.when(step == pl.num_programs(0) - 1)
    def _():
        per = LANES // cap
        for b in range(slots // LANES):
            rows = slot[:, b * LANES : (b + 1) * LANES].T
            out_ref[b * per : (b + 1) * per] = rows.reshape(per, cap, LANES).astype(BF16)


def reduce_kernel(recv_ref, slot_ref, out_ref):
    n, cap, width = slot_ref.shape
    share = recv_ref.shape[1]
    total = recv_ref[0].astype(F32)
    for d in range(1, n):
        total = total + recv_ref[d].astype(F32)
    total = total.astype(BF16)
    out_ref[:, 0:cap, :] = slot_ref[...]
    out_ref[:, cap:, :] = jnp.broadcast_to(total[None], (n, share, width))


def final_kernel(cap, recv_ref, place_ref, gws_ref, gwn_ref, gb_ref, gwc_ref, hub_ref, flat):
    n, share, width = recv_ref.shape[0], recv_ref.shape[1] - cap, recv_ref.shape[2]
    rows = recv_ref[:, 0:cap, :].astype(F32).reshape(n * cap, width).astype(BF16)
    hub_ref[...] = dot_nn(place_ref[...], rows)
    for d in range(n):
        flat[d * share : (d + 1) * share, :] = recv_ref[d, cap:, :].astype(F32)
    hidden_rows = gws_ref.shape[1]
    classes = gwc_ref.shape[0]
    class_rows = -(-classes // 16) * 16
    row = 2 * hidden_rows
    for b in range(hidden_rows // LANES):
        at = slice(b * LANES, (b + 1) * LANES)
        gws_ref[:, at] = flat[b * LANES : (b + 1) * LANES, :].T
        gwn_ref[:, at] = flat[hidden_rows + b * LANES : hidden_rows + (b + 1) * LANES, :].T
        gwc_ref[:, at] = flat[row : row + classes, :]
        row += class_rows
    gb_ref[...] = flat[row : row + hidden_rows // LANES, :]


def exchange(x):
    return lax.all_to_all(x, "dom", split_axis=0, concat_axis=0, tiled=True)


def on_device(
    feats, adj_vals, adj_cols, hub_feats, hub_mirrors, hub_links, labels, groups, train_mask,
    w_self, w_neigh, bias, w_cls, group_logw,
):
    verts, width = feats.shape
    n = lax.axis_size("dom")
    hub_dev = hub_feats.shape[0]
    mirrors = hub_mirrors.shape[1]
    links = hub_links.shape[2]
    group_total = group_logw.shape[0]
    hidden_rows, classes = w_cls.shape
    class_rows = -(-classes // 16) * 16
    row_blocks, tiles = adj_cols.shape
    cap = min(hub_dev, max(2, 2 * hub_dev * mirrors // n))
    slots = n * cap
    any_space = pl.BlockSpec(memory_space=pltpu.VMEM)
    smem = pl.BlockSpec(memory_space=pltpu.SMEM)
    sds = jax.ShapeDtypeStruct

    me = lax.axis_index("dom").reshape(1).astype(I32)
    packed, place = pl.pallas_call(
        functools.partial(pack_kernel, n, cap),
        name="pack",
        out_shape=(sds((n, cap + 2 * links, width), BF16), sds((slots, hub_dev), BF16)),
        in_specs=[smem, any_space, any_space, any_space],
        out_specs=(any_space, any_space),
        compiler_params=params(),
    )(me, off_chip(hub_feats), off_chip(hub_mirrors.T), off_chip(hub_links.transpose(1, 2, 0)))
    recv = exchange(packed)

    parts = 8
    span = parts * LANES
    steps = row_blocks // parts
    per_step = parts
    whole = lambda *shape: pl.BlockSpec(shape, lambda i, *_: (0,) * len(shape))
    s_rows, f_turned, mass, w_turned, wc_turned, wc_rows, bias_wide = pl.pallas_call(
        functools.partial(local_kernel, tiles),
        name="local",
        grid_spec=pltpu.PrefetchScalarGridSpec(
            num_scalar_prefetch=1,
            grid=(row_blocks // per_step,),
            in_specs=[
                whole(verts, width),
                pl.BlockSpec((per_step, tiles, LANES, LANES), lambda i, *_: (i, 0, 0, 0)),
                whole(width, hidden_rows),
                whole(width, hidden_rows),
                whole(classes, hidden_rows),
                whole(hidden_rows // LANES, LANES),
            ],
            out_specs=[
                pl.BlockSpec((per_step // parts, span, width), lambda i, *_: (i, 0, 0))
            ]
            + [any_space] * 4
            + [whole(hidden_rows, class_rows), any_space],
            scratch_shapes=[pltpu.VMEM((row_blocks, LANES, 2 * width), BF16)],
        ),
        out_shape=(
            pltpu.HBM((steps, span, width), F32),
            on_chip((steps, width, span), BF16),
            on_chip((steps, 1, span), F32),
            on_chip((hidden_rows, 2 * width), BF16),
            on_chip((class_rows, hidden_rows), BF16),
            pltpu.HBM((hidden_rows, class_rows), BF16),
            on_chip((hidden_rows, LANES), F32),
        ),
        compiler_params=params(1, 16),
    )(
        off_chip(adj_cols.T), off_chip(feats), off_chip(adj_vals), off_chip(w_self), off_chip(w_neigh),
        off_chip(w_cls.T), off_chip(bias.reshape(hidden_rows // LANES, LANES)),
    )

    table = (verts // LANES, LANES)
    label_table, group_table = keep(labels.reshape(table)), keep(groups.reshape(table))
    mask_table = keep(train_mask.reshape(table))
    tile_at = pl.BlockSpec((1, span, slots), lambda i: (i, 0, 0))
    agg, hid, pmo, counts, inv, group_rows, sums = pl.pallas_call(
        functools.partial(forward_kernel, n, cap, links, classes, span),
        name="forward",
        grid=(steps,),
        in_specs=[any_space, pl.BlockSpec((1, span, width), lambda i: (i, 0, 0))]
        + [any_space] * 8,
        out_specs=[any_space] * 3 + [tile_at] + [any_space] * 3,
        out_shape=(
            on_chip((steps, width, span), BF16),
            on_chip((steps, hidden_rows, span), BF16),
            on_chip((steps, class_rows, span), F32),
            pltpu.HBM((steps, span, slots), BF16),
            on_chip((steps, 1, span), F32),
            on_chip((steps, 1, span), I32),
            sds((n, 1, LANES), F32),
        ),
        scratch_shapes=[
            pltpu.VMEM((slots, 2 * width), BF16),
            pltpu.VMEM((links, slots), I32),
            pltpu.VMEM((links, slots), I32),
            pltpu.VMEM((group_total, LANES), F32),
            pltpu.VMEM((group_total, LANES), F32),
        ],
        compiler_params=params(1),
    )(
        keep(recv), off_chip(s_rows), keep(f_turned), keep(mass), label_table, group_table,
        mask_table, keep(w_turned), keep(bias_wide), keep(wc_turned),
    )
    all_sums = exchange(sums)

    grad_rows = hidden_rows // LANES * (2 * width + class_rows + 1)
    share = -(-grad_rows // (8 * n)) * 8
    message, objective, dsum = pl.pallas_call(
        functools.partial(backward_kernel, span),
        name="backward",
        grid=(steps,),
        in_specs=[any_space] * 10,
        out_specs=[any_space, smem, any_space],
        out_shape=(
            pltpu.HBM((n, share, LANES), BF16), sds((1, 1), F32), on_chip((steps, width, span), BF16),
        ),
        scratch_shapes=[
            pltpu.VMEM((group_total, LANES), F32),
            pltpu.VMEM((hidden_rows, 2 * width), F32),
            pltpu.VMEM((hidden_rows, class_rows), F32),
            pltpu.VMEM((hidden_rows, LANES), F32),
            pltpu.VMEM((n * share, LANES), F32),
        ],
        compiler_params=params(1),
    )(
        all_sums, group_logw.reshape(1, group_total), keep(pmo), keep(hid), keep(f_turned),
        keep(agg), keep(inv), keep(group_rows), keep(wc_rows), keep(w_neigh),
    )
    answer = exchange(message)

    slot_grads, place_turned = pl.pallas_call(
        slot_kernel,
        name="slots",
        grid=(steps,),
        in_specs=[any_space, tile_at, any_space],
        out_specs=[any_space] * 2,
        out_shape=(on_chip((n, cap, width), BF16), on_chip((hub_dev, slots), BF16)),
        scratch_shapes=[pltpu.VMEM((width, slots), F32)],
        compiler_params=params(1),
    )(keep(dsum), off_chip(counts), keep(place))
    reduced = pl.pallas_call(
        reduce_kernel,
        name="reduce",
        out_shape=sds((n, cap + share, LANES), BF16),
        in_specs=[any_space, any_space],
        out_specs=any_space,
        compiler_params=params(),
    )(keep(answer), keep(slot_grads))
    gathered = exchange(reduced)
    grad_w_self, grad_w_neigh, grad_bias, grad_w_cls, hub_grad = pl.pallas_call(
        functools.partial(final_kernel, cap),
        name="final",
        out_shape=(
            sds((width, hidden_rows), F32),
            sds((width, hidden_rows), F32),
            sds((hidden_rows // LANES, LANES), F32),
            sds((classes, hidden_rows), F32),
            sds((hub_dev, width), F32),
        ),
        in_specs=[any_space, any_space],
        out_specs=(any_space,) * 5,
        scratch_shapes=[pltpu.VMEM((n * share, LANES), F32)],
        compiler_params=params(),
    )(keep(gathered), keep(place_turned))
    return (
        objective.reshape(()), grad_w_self, grad_w_neigh, grad_bias.reshape(hidden_rows),
        grad_w_cls.T, hub_grad,
    )


def solution(mesh):
    in_specs = (
        P("dom", None),
        P("dom", None, None, None),
        P("dom", None),
        P("dom", None),
        P("dom", None),
        P("dom", None, None),
        P("dom"),
        P("dom"),
        P("dom"),
        P(),
        P(),
        P(),
        P(),
        P(),
    )
    out_specs = (P(), P(), P(), P(), P(), P("dom", None))
    return jax.shard_map(
        on_device, mesh=mesh, in_specs=in_specs, out_specs=out_specs, check_vma=False
    )
```

```python
import functools

import jax
import jax.numpy as jnp
from jax import lax
from jax.experimental import pallas as pl
from jax.experimental.pallas import tpu as pltpu
from jax.sharding import PartitionSpec as P

drift_rate = 0.5
LANES = 128
F32 = jnp.float32
BF16 = jnp.bfloat16
I32 = jnp.int32


def dot_nn(a, b):
    return lax.dot_general(a, b, (((1,), (0,)), ((), ())), preferred_element_type=F32)


def dot_nt(a, b):
    return lax.dot_general(a, b, (((1,), (1,)), ((), ())), preferred_element_type=F32)


def dot_tn(a, b):
    return lax.dot_general(a, b, (((0,), (0,)), ((), ())), preferred_element_type=F32)


def iota(shape, dim):
    return lax.broadcasted_iota(I32, shape, dim)


on_chip = pltpu.VMEM


def keep(x):
    return pltpu.with_memory_space_constraint(x, pltpu.VMEM)


def off_chip(x):
    return pltpu.with_memory_space_constraint(x, pltpu.HBM)


def params(n_grid=0, mib=20):
    kw = {} if n_grid == 0 else {"dimension_semantics": ("arbitrary",) * n_grid}
    return pltpu.CompilerParams(vmem_limit_bytes=mib << 20, **kw)


def pack_kernel(n, cap, hub_ref, mir_ref, link_ref, out_ref, place_ref):
    hubs, width = hub_ref.shape
    mirrors, links = link_ref.shape[0], link_ref.shape[1]
    dest = iota((n, hubs), 0)
    present = jnp.zeros((n, hubs), F32)
    for j in range(mirrors):
        present = present + jnp.where(mir_ref[j : j + 1, :] == dest, 1.0, 0.0)
    before = jnp.where(iota((hubs, hubs), 0) < iota((hubs, hubs), 1), 1.0, 0.0)
    rank = dot_nn(present.astype(BF16), before.astype(BF16))
    rank = jnp.where(present > 0.0, rank, 9999.0).astype(I32)
    place = jnp.where(rank[:, None, :] == iota((n, cap, hubs), 1), 1.0, 0.0)
    flat_place = place.reshape(n * cap, hubs).astype(BF16)
    place_ref[...] = flat_place
    rows = dot_nn(flat_place, hub_ref[...])
    out_ref[:, 0:cap, :] = rows.reshape(n, cap, width).astype(BF16)
    dest3 = iota((n, links, hubs), 0)
    ends = jnp.zeros((n, links, hubs), I32)
    for j in range(mirrors):
        ends = ends + jnp.where(mir_ref[j : j + 1, :][None] == dest3, link_ref[j][None], 0)
    high = ((ends >> 7) + 1).astype(F32)
    low = (ends & 127).astype(F32)
    both = jnp.concatenate([high, low], axis=1).astype(BF16)
    packed = lax.dot_general(
        both, place.astype(BF16), (((2,), (2,)), ((0,), (0,))), preferred_element_type=F32
    )
    rows = 2 * links * cap // LANES
    lanes = [packed[:, q * rows : (q + 1) * rows, :] for q in range(LANES // cap)]
    out_ref[:, cap : cap + rows, :] = jnp.concatenate(lanes, axis=2).astype(BF16)


def to_row(block):
    eye = iota(block.shape, 0) == iota(block.shape, 1)
    return jnp.sum(jnp.where(eye, block, 0.0), axis=0, keepdims=True)


def to_column(row):
    eye = iota((LANES, LANES), 0) == iota((LANES, LANES), 1)
    return jnp.sum(jnp.where(eye, row, 0.0), axis=1, keepdims=True)


def turn(x):
    return x.astype(F32).T


def local_kernel(
    tiles, cols_ref, feats_ref, vals_ref, ws_ref, wn_ref, wc_ref, bias_ref,
    s_ref, ft_ref, mass_ref, w_ref, wct_ref, wcn_ref, biasb_ref, wide,
):
    step = pl.program_id(0)
    width = feats_ref.shape[1]
    blocks = wide.shape[0]
    hidden_rows = ws_ref.shape[1]
    classes = wc_ref.shape[0]
    class_rows = wct_ref.shape[0]

    @pl.when(step == 0)
    def _():
        def fill(b, carry):
            wide[b, :, 0:width] = feats_ref[pl.ds(pl.multiple_of(b * LANES, LANES), LANES), :]
            wide[b, :, width:] = jnp.ones((LANES, LANES), BF16)
            return carry

        lax.fori_loop(0, blocks, fill, 0, unroll=4)
        wct_ref[...] = jnp.zeros_like(wct_ref)
        wct_ref[0:classes, :] = wc_ref[...]
        for b in range(hidden_rows // LANES):
            at = slice(b * LANES, (b + 1) * LANES)
            w_ref[at, 0:width] = turn(ws_ref[:, at]).astype(BF16)
            w_ref[at, width:] = turn(wn_ref[:, at]).astype(BF16)
            wcn_ref[at, :] = turn(wct_ref[:, at]).astype(BF16)
            biasb_ref[at, :] = jnp.broadcast_to(to_column(bias_ref[b : b + 1, :]), (LANES, LANES))

    per_step = vals_ref.shape[0]
    parts = s_ref.shape[2] // LANES
    for r in range(per_step):
        block = step * per_step + r
        home, part = step * (per_step // parts) + r // parts, r % parts
        span = slice(part * LANES, (part + 1) * LANES)
        left = jnp.concatenate([vals_ref[r, k] for k in range(tiles)], axis=1)
        right = jnp.concatenate([wide[cols_ref[k, block]] for k in range(tiles)], axis=0)
        both = dot_nn(left, right)
        own = wide[block, :, 0:width].astype(F32).T
        s_ref[r // parts, :, span] = own + both[:, 0:width].T
        ft_ref[home, :, span] = own.astype(BF16)
        mass_ref[home, :, span] = to_row(both[:, width : width + LANES])


def lane_row(ref, step, parts):
    return jnp.concatenate([ref[pl.ds(step * parts + k, 1), :] for k in range(parts)], axis=1)


def fold_lanes(x):
    total = x[:, 0:LANES]
    for k in range(1, x.shape[1] // LANES):
        total = total + x[:, k * LANES : (k + 1) * LANES]
    return total


def forward_kernel(
    n, cap, links, classes, span,
    recv_ref, s_ref, ft_ref, mass_ref, label_ref, group_ref, mask_ref, w_ref, bias_ref, wc_ref,
    agg_ref, hid_ref, pmo_ref, m_ref, inv_ref, of_ref, sums_ref,
    src, word_of, value_of, loss_acc, count_acc,
):
    step = pl.program_id(0)
    slots = n * cap
    width = s_ref.shape[1]
    groups = loss_acc.shape[0]
    parts = span // LANES

    @pl.when(step == 0)
    def _():
        loss_acc[...] = jnp.zeros_like(loss_acc)
        count_acc[...] = jnp.zeros_like(count_acc)
        per = LANES // cap
        rows = 2 * links // per
        block_of = iota((1, 1, LANES), 2) // cap
        ends = recv_ref[:, cap : cap + rows, :].astype(F32).reshape(n // per, per, rows, LANES)
        ends = [ends[:, k] for k in range(per)]
        turned = [[pltpu.roll(e, t * cap, 2) if t else e for t in range(per)] for e in ends]
        values = []
        for q in range(per):
            value = jnp.zeros((n // per, rows, LANES), F32)
            for k in range(per):
                value = jnp.where(block_of == k, turned[k][(k - q) % per], value)
            values.append(value)
        ends = jnp.concatenate(values, axis=1)
        for b in range(slots // LANES):
            at = slice(b * LANES, (b + 1) * LANES)
            rows = recv_ref[b * per : (b + 1) * per, 0:cap, :].astype(F32).reshape(LANES, width)
            src[0:width, at] = rows.T.astype(BF16)
            target = ((ends[b, 0:links] - 1.0) * 128.0 + ends[b, links:]).astype(I32)
            word_of[:, at] = (target >> 7) * 16 + (target & 15)
            value_of[:, at] = jnp.left_shift(1, ((target >> 4) & 7) * 4)
        src[width:, :] = jnp.ones((16, slots), BF16)

    chunk = 256
    for c in range(slots // chunk):
        at = slice(c * chunk, (c + 1) * chunk)
        word = [jnp.broadcast_to(word_of[k : k + 1, at], (16, chunk)) for k in range(links)]
        value = [jnp.broadcast_to(value_of[k : k + 1, at], (16, chunk)) for k in range(links)]
        for b in range(parts):
            rows16 = iota((16, chunk), 0) + (step * parts + b) * 16
            fields = jnp.zeros((16, chunk), I32)
            for k in range(links):
                fields = fields + jnp.where(word[k] == rows16, value[k], 0)
            for f in range(8):
                first = b * LANES + f * 16
                count = (fields >> (4 * f)) & 15
                m_ref[0, first : first + 16, at] = count.astype(F32).astype(BF16)
    hub = dot_nt(src[...], m_ref[0])
    inverse = 1.0 / (1.0 + mass_ref[step] + hub[width : width + 1, :])
    inv_ref[step] = inverse
    agg_ref[step] = ((s_ref[0] + hub[0:width]) * inverse).astype(BF16)
    bias = jnp.concatenate([bias_ref[...]] * parts, axis=1)
    both = jnp.concatenate([ft_ref[step], agg_ref[step]], axis=0)
    pre = dot_nn(w_ref[...], both) + bias
    hidden = jnp.maximum(pre, 0.0).astype(BF16)
    hid_ref[step] = hidden
    logits = dot_nn(wc_ref[...], hidden)
    class_row = iota(logits.shape, 0)
    logits = jnp.where(class_row < classes, logits, -jnp.inf)
    top = jnp.max(logits, axis=0, keepdims=True)
    shifted = jnp.exp(logits - top)
    total = jnp.sum(shifted, axis=0, keepdims=True)
    mask = lane_row(mask_ref, step, parts).astype(F32)
    hot = class_row == lane_row(label_ref, step, parts)
    picked = jnp.sum(jnp.where(hot, logits, 0.0), axis=0, keepdims=True)
    loss = (top + jnp.log(total) - picked) * mask
    pmo_ref[step] = mask * (shifted * (1.0 / total) - jnp.where(hot, 1.0, 0.0))
    group_row = lane_row(group_ref, step, parts)
    of_ref[step] = group_row
    in_group = iota((groups, span), 0) == group_row
    loss_acc[...] += fold_lanes(jnp.where(in_group, loss, 0.0))
    count_acc[...] += fold_lanes(jnp.where(in_group, mask, 0.0))

    @pl.when(step == pl.num_programs(0) - 1)
    def _():
        sub, lane = iota((groups, LANES), 0), iota((groups, LANES), 1)
        loss_col = jnp.sum(loss_acc[...], axis=1, keepdims=True)
        count_col = jnp.sum(count_acc[...], axis=1, keepdims=True)
        both = jnp.where(lane == sub, loss_col, 0.0) + jnp.where(
            lane == sub + groups, count_col, 0.0
        )
        row = jnp.sum(both, axis=0, keepdims=True)
        sums_ref[...] = jnp.broadcast_to(row[None], sums_ref.shape)


def backward_kernel(
    span,
    sums_ref, logw_ref, pmo_ref, hid_ref, ft_ref, agg_ref, inv_ref, group_ref, wc_ref, wn_ref,
    msg_ref, obj_ref, dsum_ref,
    q_col, gw, gwc, gb, flat,
):
    step = pl.program_id(0)
    n, share = msg_ref.shape[0], msg_ref.shape[1]
    groups = logw_ref.shape[1]
    hidden_rows = gb.shape[0]
    class_rows = pmo_ref.shape[1]

    @pl.when(step == 0)
    def _():
        row = jnp.sum(sums_ref[...], axis=0)
        sub, lane = iota((groups, LANES), 0), iota((groups, LANES), 1)
        gsum = jnp.sum(jnp.where(lane == sub, row, 0.0), axis=1, keepdims=True)
        gcount = jnp.sum(jnp.where(lane == sub + groups, row, 0.0), axis=1, keepdims=True)
        sub, lane = iota((groups, groups), 0), iota((groups, groups), 1)
        logw = jnp.sum(jnp.where(lane == sub, logw_ref[...], 0.0), axis=1, keepdims=True)
        score = logw + drift_rate * gsum / (gcount + 1.0)
        e = jnp.exp(score - jnp.max(score, axis=0, keepdims=True))
        q = groups * (e / jnp.sum(e, axis=0, keepdims=True))
        obj_ref[0, 0] = jnp.sum(q * gsum)
        q_col[...] = jnp.broadcast_to(q, q_col.shape)
        gw[...] = jnp.zeros_like(gw)
        gwc[...] = jnp.zeros_like(gwc)
        gb[...] = jnp.zeros_like(gb)

    in_group = iota((groups, span), 0) == group_ref[step]
    weight = jnp.sum(jnp.where(in_group, q_col[:, 0:1], 0.0), axis=0, keepdims=True)
    dlogits = (pmo_ref[step] * weight).astype(BF16)
    hidden = hid_ref[step]
    gwc[...] += dot_nt(hidden, dlogits)
    dhidden = dot_nn(wc_ref[...], dlogits)
    live = hidden > 0
    gb[...] += fold_lanes(jnp.where(live, dhidden, 0.0))
    dpre = jnp.where(live, dhidden.astype(BF16), jnp.zeros_like(hidden))
    gw[...] += dot_nt(dpre, jnp.concatenate([ft_ref[step], agg_ref[step]], axis=0))
    dagg = dot_nn(wn_ref[...], dpre)
    dsum_ref[step] = (dagg * inv_ref[step]).astype(BF16)

    @pl.when(step == pl.num_programs(0) - 1)
    def _():
        row = 0
        for b in range(gw.shape[1] // LANES):
            flat[row : row + hidden_rows, :] = gw[:, b * LANES : (b + 1) * LANES]
            row += hidden_rows
        for b in range(hidden_rows // LANES):
            flat[row : row + class_rows, :] = gwc[b * LANES : (b + 1) * LANES, :].T
            row += class_rows
        flat[row:, :] = jnp.zeros((flat.shape[0] - row, LANES), F32)
        for b in range(hidden_rows // LANES):
            col = jnp.sum(gb[b * LANES : (b + 1) * LANES, :], axis=1, keepdims=True)
            flat[row + b : row + b + 1, :] = to_row(jnp.broadcast_to(col, (LANES, LANES)))
        for d in range(n):
            msg_ref[d] = flat[d * share : (d + 1) * share, :].astype(BF16)


def slot_kernel(dsum_ref, m_ref, place_ref, out_ref, turned_ref, slot):
    step = pl.program_id(0)
    n, cap = out_ref.shape[0], out_ref.shape[1]
    slots = n * cap

    @pl.when(step == 0)
    def _():
        slot[...] = jnp.zeros_like(slot)
        for b in range(slots // LANES):
            at = slice(b * LANES, (b + 1) * LANES)
            turned_ref[:, at] = turn(place_ref[at, :]).astype(BF16)

    slot[...] += dot_nn(dsum_ref[step], m_ref[0])

    @pl.when(step == pl.num_programs(0) - 1)
    def _():
        per = LANES // cap
        for b in range(slots // LANES):
            rows = slot[:, b * LANES : (b + 1) * LANES].T
            out_ref[b * per : (b + 1) * per] = rows.reshape(per, cap, LANES).astype(BF16)


def reduce_kernel(recv_ref, slot_ref, out_ref):
    n, cap, width = slot_ref.shape
    share = recv_ref.shape[1]
    total = recv_ref[0].astype(F32)
    for d in range(1, n):
        total = total + recv_ref[d].astype(F32)
    total = total.astype(BF16)
    out_ref[:, 0:cap, :] = slot_ref[...]
    out_ref[:, cap:, :] = jnp.broadcast_to(total[None], (n, share, width))


def final_kernel(cap, recv_ref, place_ref, gws_ref, gwn_ref, gb_ref, gwc_ref, hub_ref, flat):
    n, share, width = recv_ref.shape[0], recv_ref.shape[1] - cap, recv_ref.shape[2]
    rows = recv_ref[:, 0:cap, :].astype(F32).reshape(n * cap, width).astype(BF16)
    hub_ref[...] = dot_nn(place_ref[...], rows)
    for d in range(n):
        flat[d * share : (d + 1) * share, :] = recv_ref[d, cap:, :].astype(F32)
    hidden_rows = gws_ref.shape[1]
    classes = gwc_ref.shape[0]
    class_rows = -(-classes // 16) * 16
    row = 2 * hidden_rows
    for b in range(hidden_rows // LANES):
        at = slice(b * LANES, (b + 1) * LANES)
        gws_ref[:, at] = flat[b * LANES : (b + 1) * LANES, :].T
        gwn_ref[:, at] = flat[hidden_rows + b * LANES : hidden_rows + (b + 1) * LANES, :].T
        gwc_ref[:, at] = flat[row : row + classes, :]
        row += class_rows
    gb_ref[...] = flat[row : row + hidden_rows // LANES, :]


def exchange(x):
    return lax.all_to_all(x, "dom", split_axis=0, concat_axis=0, tiled=True)


def on_device(
    feats, adj_vals, adj_cols, hub_feats, hub_mirrors, hub_links, labels, groups, train_mask,
    w_self, w_neigh, bias, w_cls, group_logw,
):
    verts, width = feats.shape
    n = lax.axis_size("dom")
    hub_dev = hub_feats.shape[0]
    mirrors = hub_mirrors.shape[1]
    links = hub_links.shape[2]
    group_total = group_logw.shape[0]
    hidden_rows, classes = w_cls.shape
    class_rows = -(-classes // 16) * 16
    row_blocks, tiles = adj_cols.shape
    cap = min(hub_dev, max(2, 2 * hub_dev * mirrors // n))
    slots = n * cap
    any_space = pl.BlockSpec(memory_space=pltpu.VMEM)
    smem = pl.BlockSpec(memory_space=pltpu.SMEM)
    sds = jax.ShapeDtypeStruct

    link_rows = 2 * links * cap // LANES
    packed, place = pl.pallas_call(
        functools.partial(pack_kernel, n, cap),
        name="pack",
        out_shape=(sds((n, cap + link_rows, width), BF16), sds((slots, hub_dev), BF16)),
        in_specs=[any_space, any_space, any_space],
        out_specs=(any_space, any_space),
        compiler_params=params(),
    )(off_chip(hub_feats), off_chip(hub_mirrors.T), off_chip(hub_links.transpose(1, 2, 0)))
    recv = exchange(packed)

    parts = 8
    span = parts * LANES
    steps = row_blocks // parts
    per_step = parts
    whole = lambda *shape: pl.BlockSpec(shape, lambda i, *_: (0,) * len(shape))
    s_rows, f_turned, mass, w_turned, wc_turned, wc_rows, bias_wide = pl.pallas_call(
        functools.partial(local_kernel, tiles),
        name="local",
        grid_spec=pltpu.PrefetchScalarGridSpec(
            num_scalar_prefetch=1,
            grid=(row_blocks // per_step,),
            in_specs=[
                whole(verts, width),
                pl.BlockSpec((per_step, tiles, LANES, LANES), lambda i, *_: (i, 0, 0, 0)),
                whole(width, hidden_rows),
                whole(width, hidden_rows),
                whole(classes, hidden_rows),
                whole(hidden_rows // LANES, LANES),
            ],
            out_specs=[
                pl.BlockSpec((per_step // parts, width, span), lambda i, *_: (i, 0, 0))
            ]
            + [any_space] * 4
            + [whole(hidden_rows, class_rows), any_space],
            scratch_shapes=[pltpu.VMEM((row_blocks, LANES, 2 * width), BF16)],
        ),
        out_shape=(
            pltpu.HBM((steps, width, span), F32),
            on_chip((steps, width, span), BF16),
            on_chip((steps, 1, span), F32),
            on_chip((hidden_rows, 2 * width), BF16),
            on_chip((class_rows, hidden_rows), BF16),
            pltpu.HBM((hidden_rows, class_rows), BF16),
            on_chip((hidden_rows, LANES), F32),
        ),
        compiler_params=params(1, 16),
    )(
        off_chip(adj_cols.T), off_chip(feats), off_chip(adj_vals), off_chip(w_self), off_chip(w_neigh),
        off_chip(w_cls.T), off_chip(bias.reshape(hidden_rows // LANES, LANES)),
    )

    table = (verts // LANES, LANES)
    label_table, group_table = keep(labels.reshape(table)), keep(groups.reshape(table))
    mask_table = keep(train_mask.reshape(table))
    tile_at = pl.BlockSpec((1, span, slots), lambda i: (i, 0, 0))
    agg, hid, pmo, counts, inv, group_rows, sums = pl.pallas_call(
        functools.partial(forward_kernel, n, cap, links, classes, span),
        name="forward",
        grid=(steps,),
        in_specs=[any_space, pl.BlockSpec((1, width, span), lambda i: (i, 0, 0))]
        + [any_space] * 8,
        out_specs=[any_space] * 3 + [tile_at] + [any_space] * 3,
        out_shape=(
            on_chip((steps, width, span), BF16),
            on_chip((steps, hidden_rows, span), BF16),
            on_chip((steps, class_rows, span), F32),
            pltpu.HBM((steps, span, slots), BF16),
            on_chip((steps, 1, span), F32),
            on_chip((steps, 1, span), I32),
            sds((n, 1, LANES), F32),
        ),
        scratch_shapes=[
            pltpu.VMEM((width + 16, slots), BF16),
            pltpu.VMEM((links, slots), I32),
            pltpu.VMEM((links, slots), I32),
            pltpu.VMEM((group_total, LANES), F32),
            pltpu.VMEM((group_total, LANES), F32),
        ],
        compiler_params=params(1),
    )(
        keep(recv), off_chip(s_rows), keep(f_turned), keep(mass), label_table, group_table,
        mask_table, keep(w_turned), keep(bias_wide), keep(wc_turned),
    )
    all_sums = exchange(sums)

    grad_rows = hidden_rows // LANES * (2 * width + class_rows + 1)
    share = -(-grad_rows // (8 * n)) * 8
    message, objective, dsum = pl.pallas_call(
        functools.partial(backward_kernel, span),
        name="backward",
        grid=(steps,),
        in_specs=[any_space] * 10,
        out_specs=[any_space, smem, any_space],
        out_shape=(
            pltpu.HBM((n, share, LANES), BF16), sds((1, 1), F32), on_chip((steps, width, span), BF16),
        ),
        scratch_shapes=[
            pltpu.VMEM((group_total, LANES), F32),
            pltpu.VMEM((hidden_rows, 2 * width), F32),
            pltpu.VMEM((hidden_rows, class_rows), F32),
            pltpu.VMEM((hidden_rows, LANES), F32),
            pltpu.VMEM((n * share, LANES), F32),
        ],
        compiler_params=params(1),
    )(
        all_sums, group_logw.reshape(1, group_total), keep(pmo), keep(hid), keep(f_turned),
        keep(agg), keep(inv), keep(group_rows), keep(wc_rows), keep(w_neigh),
    )
    answer = exchange(message)

    slot_grads, place_turned = pl.pallas_call(
        slot_kernel,
        name="slots",
        grid=(steps,),
        in_specs=[any_space, tile_at, any_space],
        out_specs=[any_space] * 2,
        out_shape=(on_chip((n, cap, width), BF16), on_chip((hub_dev, slots), BF16)),
        scratch_shapes=[pltpu.VMEM((width, slots), F32)],
        compiler_params=params(1),
    )(keep(dsum), off_chip(counts), keep(place))
    reduced = pl.pallas_call(
        reduce_kernel,
        name="reduce",
        out_shape=sds((n, cap + share, LANES), BF16),
        in_specs=[any_space, any_space],
        out_specs=any_space,
        compiler_params=params(),
    )(keep(answer), keep(slot_grads))
    gathered = exchange(reduced)
    grad_w_self, grad_w_neigh, grad_bias, grad_w_cls, hub_grad = pl.pallas_call(
        functools.partial(final_kernel, cap),
        name="final",
        out_shape=(
            sds((width, hidden_rows), F32),
            sds((width, hidden_rows), F32),
            sds((hidden_rows // LANES, LANES), F32),
            sds((classes, hidden_rows), F32),
            sds((hub_dev, width), F32),
        ),
        in_specs=[any_space, any_space],
        out_specs=(any_space,) * 5,
        scratch_shapes=[pltpu.VMEM((n * share, LANES), F32)],
        compiler_params=params(),
    )(keep(gathered), keep(place_turned))
    return (
        objective.reshape(()), grad_w_self, grad_w_neigh, grad_bias.reshape(hidden_rows),
        grad_w_cls.T, hub_grad,
    )


def solution(mesh):
    in_specs = (
        P("dom", None),
        P("dom", None, None, None),
        P("dom", None),
        P("dom", None),
        P("dom", None),
        P("dom", None, None),
        P("dom"),
        P("dom"),
        P("dom"),
        P(),
        P(),
        P(),
        P(),
        P(),
    )
    out_specs = (P(), P(), P(), P(), P(), P("dom", None))
    return jax.shard_map(
        on_device, mesh=mesh, in_specs=in_specs, out_specs=out_specs, check_vma=False
    )
```

```python
import functools

import jax
import jax.numpy as jnp
from jax import lax
from jax.experimental import pallas as pl
from jax.experimental.pallas import tpu as pltpu
from jax.sharding import PartitionSpec as P

drift_rate = 0.5
LANES = 128
F32 = jnp.float32
BF16 = jnp.bfloat16
I32 = jnp.int32


def dot_nn(a, b):
    return lax.dot_general(a, b, (((1,), (0,)), ((), ())), preferred_element_type=F32)


def dot_nt(a, b):
    return lax.dot_general(a, b, (((1,), (1,)), ((), ())), preferred_element_type=F32)


def dot_tn(a, b):
    return lax.dot_general(a, b, (((0,), (0,)), ((), ())), preferred_element_type=F32)


def iota(shape, dim):
    return lax.broadcasted_iota(I32, shape, dim)


on_chip = pltpu.VMEM


def keep(x):
    return pltpu.with_memory_space_constraint(x, pltpu.VMEM)


def off_chip(x):
    return pltpu.with_memory_space_constraint(x, pltpu.HBM)


def params(n_grid=0, mib=20):
    kw = {} if n_grid == 0 else {"dimension_semantics": ("arbitrary",) * n_grid}
    return pltpu.CompilerParams(vmem_limit_bytes=mib << 20, **kw)


def pack_kernel(n, cap, _, hub_ref, mir_ref, link_ref, out_ref, place_ref):
    hubs, width = hub_ref.shape
    mirrors, links = link_ref.shape[0], link_ref.shape[1]
    dest = iota((n, hubs), 0)
    present = jnp.zeros((n, hubs), F32)
    for j in range(mirrors):
        present = present + jnp.where(mir_ref[j : j + 1, :] == dest, 1.0, 0.0)
    before = jnp.where(iota((hubs, hubs), 0) < iota((hubs, hubs), 1), 1.0, 0.0)
    rank = dot_nn(present.astype(BF16), before.astype(BF16))
    rank = jnp.where(present > 0.0, rank, 9999.0).astype(I32)
    place = jnp.where(rank[:, None, :] == iota((n, cap, hubs), 1), 1.0, 0.0)
    flat_place = place.reshape(n * cap, hubs).astype(BF16)
    place_ref[...] = flat_place
    rows = dot_nn(flat_place, hub_ref[...])
    out_ref[:, 0:cap, :] = rows.reshape(n, cap, width).astype(BF16)
    dest3 = iota((n, links, hubs), 0)
    ends = jnp.zeros((n, links, hubs), I32)
    for j in range(mirrors):
        ends = ends + jnp.where(mir_ref[j : j + 1, :][None] == dest3, link_ref[j][None], 0)
    high = ((ends >> 7) + 1).astype(F32)
    low = (ends & 127).astype(F32)
    both = jnp.concatenate([high, low], axis=1).astype(BF16)
    packed = lax.dot_general(
        both, place.astype(BF16), (((2,), (2,)), ((0,), (0,))), preferred_element_type=F32
    )
    rows = 2 * links * cap // LANES
    lanes = [packed[:, q * rows : (q + 1) * rows, :] for q in range(LANES // cap)]
    out_ref[:, cap : cap + rows, :] = jnp.concatenate(lanes, axis=2).astype(BF16)


def to_row(block):
    eye = iota(block.shape, 0) == iota(block.shape, 1)
    return jnp.sum(jnp.where(eye, block, 0.0), axis=0, keepdims=True)


def to_column(row):
    eye = iota((LANES, LANES), 0) == iota((LANES, LANES), 1)
    return jnp.sum(jnp.where(eye, row, 0.0), axis=1, keepdims=True)


def turn(x):
    return x.astype(F32).T


def local_kernel(
    tiles, cols_ref, feats_ref, vals_ref, ws_ref, wn_ref, wc_ref, bias_ref,
    s_ref, ft_ref, mass_ref, w_ref, wct_ref, wcn_ref, biasb_ref, wide,
):
    step = pl.program_id(0)
    width = feats_ref.shape[1]
    blocks = wide.shape[0]
    hidden_rows = ws_ref.shape[1]
    classes = wc_ref.shape[0]
    class_rows = wct_ref.shape[0]

    @pl.when(step == 0)
    def _():
        def fill(b, carry):
            wide[b, :, 0:width] = feats_ref[pl.ds(pl.multiple_of(b * LANES, LANES), LANES), :]
            wide[b, :, width:] = jnp.ones((LANES, LANES), BF16)
            return carry

        lax.fori_loop(0, blocks, fill, 0, unroll=4)
        wct_ref[...] = jnp.zeros_like(wct_ref)
        wct_ref[0:classes, :] = wc_ref[...]
        for b in range(hidden_rows // LANES):
            at = slice(b * LANES, (b + 1) * LANES)
            w_ref[at, 0:width] = turn(ws_ref[:, at]).astype(BF16)
            w_ref[at, width:] = turn(wn_ref[:, at]).astype(BF16)
            wcn_ref[at, :] = turn(wct_ref[:, at]).astype(BF16)
            biasb_ref[at, :] = jnp.broadcast_to(to_column(bias_ref[b : b + 1, :]), (LANES, LANES))

    per_step = vals_ref.shape[0]
    parts = s_ref.shape[2] // LANES
    for r in range(per_step):
        block = step * per_step + r
        home, part = step * (per_step // parts) + r // parts, r % parts
        span = slice(part * LANES, (part + 1) * LANES)
        left = jnp.concatenate([vals_ref[r, k] for k in range(tiles)], axis=1)
        right = jnp.concatenate([wide[cols_ref[k, block]] for k in range(tiles)], axis=0)
        both = dot_nn(left, right)
        own = wide[block, :, 0:width].astype(F32).T
        s_ref[r // parts, :, span] = own + both[:, 0:width].T
        ft_ref[home, :, span] = own.astype(BF16)
        mass_ref[home, :, span] = to_row(both[:, width : width + LANES])


def lane_row(ref, step, parts):
    return jnp.concatenate([ref[pl.ds(step * parts + k, 1), :] for k in range(parts)], axis=1)


def fold_lanes(x):
    total = x[:, 0:LANES]
    for k in range(1, x.shape[1] // LANES):
        total = total + x[:, k * LANES : (k + 1) * LANES]
    return total


def forward_kernel(
    n, cap, links, classes, span,
    recv_ref, s_ref, ft_ref, mass_ref, label_ref, group_ref, mask_ref, w_ref, bias_ref, wc_ref,
    agg_ref, hid_ref, pmo_ref, m_ref, inv_ref, of_ref, sums_ref,
    src, word_of, value_of, loss_acc, count_acc,
):
    step = pl.program_id(0)
    slots = n * cap
    width = s_ref.shape[1]
    groups = loss_acc.shape[0]
    parts = span // LANES

    @pl.when(step == 0)
    def _():
        loss_acc[...] = jnp.zeros_like(loss_acc)
        count_acc[...] = jnp.zeros_like(count_acc)
        per = LANES // cap
        rows = 2 * links // per
        block_of = iota((1, 1, LANES), 2) // cap
        ends = recv_ref[:, cap : cap + rows, :].astype(F32).reshape(n // per, per, rows, LANES)
        ends = [ends[:, k] for k in range(per)]
        turned = [[pltpu.roll(e, t * cap, 2) if t else e for t in range(per)] for e in ends]
        values = []
        for q in range(per):
            value = jnp.zeros((n // per, rows, LANES), F32)
            for k in range(per):
                value = jnp.where(block_of == k, turned[k][(k - q) % per], value)
            values.append(value)
        ends = jnp.concatenate(values, axis=1)
        for b in range(slots // LANES):
            at = slice(b * LANES, (b + 1) * LANES)
            rows = recv_ref[b * per : (b + 1) * per, 0:cap, :].astype(F32).reshape(LANES, width)
            src[0:width, at] = rows.T.astype(BF16)
            target = ((ends[b, 0:links] - 1.0) * 128.0 + ends[b, links:]).astype(I32)
            word_of[:, at] = (target >> 7) * 16 + (target & 15)
            value_of[:, at] = jnp.left_shift(1, ((target >> 4) & 7) * 4)
        src[width:, :] = jnp.ones((16, slots), BF16)

    chunk = 256
    for c in range(slots // chunk):
        at = slice(c * chunk, (c + 1) * chunk)
        word = [jnp.broadcast_to(word_of[k : k + 1, at], (16, chunk)) for k in range(links)]
        value = [jnp.broadcast_to(value_of[k : k + 1, at], (16, chunk)) for k in range(links)]
        for b in range(parts):
            rows16 = iota((16, chunk), 0) + (step * parts + b) * 16
            fields = jnp.zeros((16, chunk), I32)
            for k in range(links):
                fields = fields + jnp.where(word[k] == rows16, value[k], 0)
            for f in range(8):
                first = b * LANES + f * 16
                count = (fields >> (4 * f)) & 15
                m_ref[0, first : first + 16, at] = count.astype(F32).astype(BF16)
    hub = dot_nt(src[...], m_ref[0])
    inverse = 1.0 / (1.0 + mass_ref[step] + hub[width : width + 1, :])
    inv_ref[step] = inverse
    agg_ref[step] = ((s_ref[0] + hub[0:width]) * inverse).astype(BF16)
    bias = jnp.concatenate([bias_ref[...]] * parts, axis=1)
    both = jnp.concatenate([ft_ref[step], agg_ref[step]], axis=0)
    pre = dot_nn(w_ref[...], both) + bias
    hidden = jnp.maximum(pre, 0.0).astype(BF16)
    hid_ref[step] = hidden
    logits = dot_nn(wc_ref[...], hidden)
    class_row = iota(logits.shape, 0)
    logits = jnp.where(class_row < classes, logits, -jnp.inf)
    top = jnp.max(logits, axis=0, keepdims=True)
    shifted = jnp.exp(logits - top)
    total = jnp.sum(shifted, axis=0, keepdims=True)
    mask = lane_row(mask_ref, step, parts).astype(F32)
    hot = class_row == lane_row(label_ref, step, parts)
    picked = jnp.sum(jnp.where(hot, logits, 0.0), axis=0, keepdims=True)
    loss = (top + jnp.log(total) - picked) * mask
    pmo_ref[step] = shifted * (mask / total) - jnp.where(hot, mask, 0.0)
    group_row = lane_row(group_ref, step, parts)
    of_ref[step] = group_row
    in_group = iota((groups, span), 0) == group_row
    loss_acc[...] += fold_lanes(jnp.where(in_group, loss, 0.0))
    count_acc[...] += fold_lanes(jnp.where(in_group, mask, 0.0))

    @pl.when(step == pl.num_programs(0) - 1)
    def _():
        sub, lane = iota((groups, LANES), 0), iota((groups, LANES), 1)
        loss_col = jnp.sum(loss_acc[...], axis=1, keepdims=True)
        count_col = jnp.sum(count_acc[...], axis=1, keepdims=True)
        both = jnp.where(lane == sub, loss_col, 0.0) + jnp.where(
            lane == sub + groups, count_col, 0.0
        )
        row = jnp.sum(both, axis=0, keepdims=True)
        sums_ref[...] = jnp.broadcast_to(row[None], sums_ref.shape)


def backward_kernel(
    span,
    me_ref, sums_ref, logw_ref, pmo_ref, hid_ref, ft_ref, agg_ref, inv_ref, group_ref, wc_ref, wn_ref,
    own_ref, pass_ref, obj_ref, dsum_ref,
    q_col, gw, gwc, gb, flat,
):
    step = pl.program_id(0)
    half, share = pass_ref.shape[0], pass_ref.shape[1]
    groups = logw_ref.shape[1]
    hidden_rows = gb.shape[0]
    class_rows = pmo_ref.shape[1]

    @pl.when(step == 0)
    def _():
        row = jnp.sum(sums_ref[...], axis=0)
        sub, lane = iota((groups, LANES), 0), iota((groups, LANES), 1)
        gsum = jnp.sum(jnp.where(lane == sub, row, 0.0), axis=1, keepdims=True)
        gcount = jnp.sum(jnp.where(lane == sub + groups, row, 0.0), axis=1, keepdims=True)
        sub, lane = iota((groups, groups), 0), iota((groups, groups), 1)
        logw = jnp.sum(jnp.where(lane == sub, logw_ref[...], 0.0), axis=1, keepdims=True)
        score = logw + drift_rate * gsum / (gcount + 1.0)
        e = jnp.exp(score - jnp.max(score, axis=0, keepdims=True))
        q = groups * (e / jnp.sum(e, axis=0, keepdims=True))
        obj_ref[0, 0] = jnp.sum(q * gsum)
        q_col[...] = jnp.broadcast_to(q, q_col.shape)
        gw[...] = jnp.zeros_like(gw)
        gwc[...] = jnp.zeros_like(gwc)
        gb[...] = jnp.zeros_like(gb)

    in_group = iota((groups, span), 0) == group_ref[step]
    weight = jnp.sum(jnp.where(in_group, q_col[:, 0:1], 0.0), axis=0, keepdims=True)
    dlogits = (pmo_ref[step] * weight).astype(BF16)
    hidden = hid_ref[step]
    gwc[...] += dot_nt(hidden, dlogits)
    dhidden = dot_nn(wc_ref[...], dlogits)
    live = hidden > 0
    gb[...] += fold_lanes(jnp.where(live, dhidden, 0.0))
    dpre = jnp.where(live, dhidden.astype(BF16), jnp.zeros_like(hidden))
    gw[...] += dot_nt(dpre, jnp.concatenate([ft_ref[step], agg_ref[step]], axis=0))
    dagg = dot_nn(wn_ref[...], dpre)
    dsum_ref[step] = (dagg * inv_ref[step]).astype(BF16)

    @pl.when(step == pl.num_programs(0) - 1)
    def _():
        row = 0
        for b in range(gw.shape[1] // LANES):
            flat[row : row + hidden_rows, :] = gw[:, b * LANES : (b + 1) * LANES]
            row += hidden_rows
        for b in range(hidden_rows // LANES):
            flat[row : row + class_rows, :] = gwc[b * LANES : (b + 1) * LANES, :].T
            row += class_rows
        flat[row:, :] = jnp.zeros((flat.shape[0] - row, LANES), F32)
        for b in range(hidden_rows // LANES):
            col = jnp.sum(gb[b * LANES : (b + 1) * LANES, :], axis=1, keepdims=True)
            flat[row + b : row + b + 1, :] = to_row(jnp.broadcast_to(col, (LANES, LANES)))
        core = me_ref[0] % 2
        for d in range(half):
            own_at = pl.multiple_of((2 * d + core) * share, 8)
            own_ref[d] = flat[pl.ds(own_at, share), :]
            pass_at = pl.multiple_of((2 * d + 1 - core) * share, 8)
            pass_ref[d] = flat[pl.ds(pass_at, share), :].astype(BF16)


def slot_kernel(dsum_ref, m_ref, place_ref, out_ref, turned_ref, slot):
    step = pl.program_id(0)
    n, cap = out_ref.shape[0], out_ref.shape[1]
    slots = n * cap

    @pl.when(step == 0)
    def _():
        slot[...] = jnp.zeros_like(slot)
        for b in range(slots // LANES):
            at = slice(b * LANES, (b + 1) * LANES)
            turned_ref[:, at] = turn(place_ref[at, :]).astype(BF16)

    total = slot[...]
    blocks = m_ref.shape[0]
    for k in range(blocks):
        total = total + dot_nn(dsum_ref[step * blocks + k], m_ref[k])
    slot[...] = total

    @pl.when(step == pl.num_programs(0) - 1)
    def _():
        per = LANES // cap
        for b in range(slots // LANES):
            rows = slot[:, b * LANES : (b + 1) * LANES].T
            out_ref[b * per : (b + 1) * per] = rows.reshape(per, cap, LANES).astype(BF16)


def pair_kernel(own_ref, recv_ref, out_ref):
    out_ref[...] = (own_ref[...] + recv_ref[...].astype(F32)).astype(BF16)


def reduce_kernel(recv_ref, slot_ref, out_ref):
    n, cap, width = slot_ref.shape
    share = recv_ref.shape[1]
    total = recv_ref[0].astype(F32)
    for d in range(1, recv_ref.shape[0]):
        total = total + recv_ref[d].astype(F32)
    total = total.astype(BF16)
    out_ref[:, 0:cap, :] = slot_ref[...]
    out_ref[:, cap:, :] = jnp.broadcast_to(total[None], (n, share, width))


def final_kernel(cap, recv_ref, place_ref, gws_ref, gwn_ref, gb_ref, gwc_ref, hub_ref, flat):
    n, share, width = recv_ref.shape[0], recv_ref.shape[1] - cap, recv_ref.shape[2]
    rows = recv_ref[:, 0:cap, :].astype(F32).reshape(n * cap, width).astype(BF16)
    hub_ref[...] = dot_nn(place_ref[...], rows)
    for d in range(n):
        flat[d * share : (d + 1) * share, :] = recv_ref[d, cap:, :].astype(F32)
    hidden_rows = gws_ref.shape[1]
    classes = gwc_ref.shape[0]
    class_rows = -(-classes // 16) * 16
    row = 2 * hidden_rows
    for b in range(hidden_rows // LANES):
        at = slice(b * LANES, (b + 1) * LANES)
        gws_ref[:, at] = flat[b * LANES : (b + 1) * LANES, :].T
        gwn_ref[:, at] = flat[hidden_rows + b * LANES : hidden_rows + (b + 1) * LANES, :].T
        gwc_ref[:, at] = flat[row : row + classes, :]
        row += class_rows
    gb_ref[...] = flat[row : row + hidden_rows // LANES, :]


def exchange(x):
    return lax.all_to_all(x, "dom", split_axis=0, concat_axis=0, tiled=True)


def on_device(
    feats, adj_vals, adj_cols, hub_feats, hub_mirrors, hub_links, labels, groups, train_mask,
    w_self, w_neigh, bias, w_cls, group_logw,
):
    verts, width = feats.shape
    n = lax.axis_size("dom")
    hub_dev = hub_feats.shape[0]
    mirrors = hub_mirrors.shape[1]
    links = hub_links.shape[2]
    group_total = group_logw.shape[0]
    hidden_rows, classes = w_cls.shape
    class_rows = -(-classes // 16) * 16
    row_blocks, tiles = adj_cols.shape
    cap = min(hub_dev, max(2, 2 * hub_dev * mirrors // n))
    slots = n * cap
    any_space = pl.BlockSpec(memory_space=pltpu.VMEM)
    smem = pl.BlockSpec(memory_space=pltpu.SMEM)
    sds = jax.ShapeDtypeStruct

    link_rows = 2 * links * cap // LANES
    me = lax.axis_index("dom").reshape(1).astype(I32)
    packed, place = pl.pallas_call(
        functools.partial(pack_kernel, n, cap),
        name="pack",
        out_shape=(sds((n, cap + link_rows, width), BF16), sds((slots, hub_dev), BF16)),
        in_specs=[smem, any_space, any_space, any_space],
        out_specs=(any_space, any_space),
        compiler_params=params(),
    )(me, off_chip(hub_feats), off_chip(hub_mirrors.T), off_chip(hub_links.transpose(1, 2, 0)))
    recv = exchange(packed)

    parts = 8
    span = parts * LANES
    steps = row_blocks // parts
    per_step = parts
    whole = lambda *shape: pl.BlockSpec(shape, lambda i, *_: (0,) * len(shape))
    s_rows, f_turned, mass, w_turned, wc_turned, wc_rows, bias_wide = pl.pallas_call(
        functools.partial(local_kernel, tiles),
        name="local",
        grid_spec=pltpu.PrefetchScalarGridSpec(
            num_scalar_prefetch=1,
            grid=(row_blocks // per_step,),
            in_specs=[
                whole(verts, width),
                pl.BlockSpec((per_step, tiles, LANES, LANES), lambda i, *_: (i, 0, 0, 0)),
                whole(width, hidden_rows),
                whole(width, hidden_rows),
                whole(classes, hidden_rows),
                whole(hidden_rows // LANES, LANES),
            ],
            out_specs=[
                pl.BlockSpec((per_step // parts, width, span), lambda i, *_: (i, 0, 0))
            ]
            + [any_space] * 4
            + [whole(hidden_rows, class_rows), any_space],
            scratch_shapes=[pltpu.VMEM((row_blocks, LANES, 2 * width), BF16)],
        ),
        out_shape=(
            pltpu.HBM((steps, width, span), F32),
            on_chip((steps, width, span), BF16),
            on_chip((steps, 1, span), F32),
            on_chip((hidden_rows, 2 * width), BF16),
            on_chip((class_rows, hidden_rows), BF16),
            pltpu.HBM((hidden_rows, class_rows), BF16),
            on_chip((hidden_rows, LANES), F32),
        ),
        compiler_params=params(1, 16),
    )(
        off_chip(adj_cols.T), off_chip(feats), off_chip(adj_vals), off_chip(w_self), off_chip(w_neigh),
        off_chip(w_cls.T), off_chip(bias.reshape(hidden_rows // LANES, LANES)),
    )

    table = (verts // LANES, LANES)
    label_table, group_table = keep(labels.reshape(table)), keep(groups.reshape(table))
    mask_table = keep(train_mask.reshape(table))
    tile_at = pl.BlockSpec((1, span, slots), lambda i: (i, 0, 0))
    agg, hid, pmo, counts, inv, group_rows, sums = pl.pallas_call(
        functools.partial(forward_kernel, n, cap, links, classes, span),
        name="forward",
        grid=(steps,),
        in_specs=[any_space, pl.BlockSpec((1, width, span), lambda i: (i, 0, 0))]
        + [any_space] * 8,
        out_specs=[any_space] * 3 + [tile_at] + [any_space] * 3,
        out_shape=(
            on_chip((steps, width, span), BF16),
            on_chip((steps, hidden_rows, span), BF16),
            on_chip((steps, class_rows, span), F32),
            pltpu.HBM((steps, span, slots), BF16),
            on_chip((steps, 1, span), F32),
            on_chip((steps, 1, span), I32),
            sds((n, 1, LANES), F32),
        ),
        scratch_shapes=[
            pltpu.VMEM((width + 16, slots), BF16),
            pltpu.VMEM((links, slots), I32),
            pltpu.VMEM((links, slots), I32),
            pltpu.VMEM((group_total, LANES), F32),
            pltpu.VMEM((group_total, LANES), F32),
        ],
        compiler_params=params(1),
    )(
        keep(recv), off_chip(s_rows), keep(f_turned), keep(mass), label_table, group_table,
        mask_table, keep(w_turned), keep(bias_wide), keep(wc_turned),
    )
    all_sums = exchange(sums)

    grad_rows = hidden_rows // LANES * (2 * width + class_rows + 1)
    share = -(-grad_rows // (8 * n)) * 8
    half = n // 2
    own, passed, objective, dsum = pl.pallas_call(
        functools.partial(backward_kernel, span),
        name="backward",
        grid=(steps,),
        in_specs=[smem] + [any_space] * 10,
        out_specs=[any_space, any_space, smem, any_space],
        out_shape=(
            on_chip((half, share, LANES), F32), pltpu.HBM((half, share, LANES), BF16),
            sds((1, 1), F32), on_chip((steps, width, span), BF16),
        ),
        scratch_shapes=[
            pltpu.VMEM((group_total, LANES), F32),
            pltpu.VMEM((hidden_rows, 2 * width), F32),
            pltpu.VMEM((hidden_rows, class_rows), F32),
            pltpu.VMEM((hidden_rows, LANES), F32),
            pltpu.VMEM((n * share, LANES), F32),
        ],
        compiler_params=params(1),
    )(
        me, all_sums, group_logw.reshape(1, group_total), keep(pmo), keep(hid), keep(f_turned),
        keep(agg), keep(inv), keep(group_rows), keep(wc_rows), keep(w_neigh),
    )
    other = lax.ppermute(passed, "dom", [(i, i ^ 1) for i in range(n)])
    paired = pl.pallas_call(
        pair_kernel,
        name="pair",
        out_shape=pltpu.HBM((half, share, LANES), BF16),
        in_specs=[any_space, any_space],
        out_specs=any_space,
        compiler_params=params(),
    )(keep(own), keep(other))
    same_core = [list(range(core, n, 2)) for core in range(2)]
    answer = lax.all_to_all(
        paired, "dom", split_axis=0, concat_axis=0, tiled=True, axis_index_groups=same_core
    )

    blocks = 2 if steps % 2 == 0 else 1
    slot_grads, place_turned = pl.pallas_call(
        slot_kernel,
        name="slots",
        grid=(steps // blocks,),
        in_specs=[any_space, pl.BlockSpec((blocks, span, slots), lambda i: (i, 0, 0)), any_space],
        out_specs=[any_space] * 2,
        out_shape=(on_chip((n, cap, width), BF16), on_chip((hub_dev, slots), BF16)),
        scratch_shapes=[pltpu.VMEM((width, slots), F32)],
        compiler_params=params(1, 20),
    )(keep(dsum), off_chip(counts), keep(place))
    reduced = pl.pallas_call(
        reduce_kernel,
        name="reduce",
        out_shape=sds((n, cap + share, LANES), BF16),
        in_specs=[any_space, any_space],
        out_specs=any_space,
        compiler_params=params(),
    )(keep(answer), keep(slot_grads))
    gathered = exchange(reduced)
    grad_w_self, grad_w_neigh, grad_bias, grad_w_cls, hub_grad = pl.pallas_call(
        functools.partial(final_kernel, cap),
        name="final",
        out_shape=(
            sds((width, hidden_rows), F32),
            sds((width, hidden_rows), F32),
            sds((hidden_rows // LANES, LANES), F32),
            sds((classes, hidden_rows), F32),
            sds((hub_dev, width), F32),
        ),
        in_specs=[any_space, any_space],
        out_specs=(any_space,) * 5,
        scratch_shapes=[pltpu.VMEM((n * share, LANES), F32)],
        compiler_params=params(),
    )(keep(gathered), keep(place_turned))
    return (
        objective.reshape(()), grad_w_self, grad_w_neigh, grad_bias.reshape(hidden_rows),
        grad_w_cls.T, hub_grad,
    )


def solution(mesh):
    in_specs = (
        P("dom", None),
        P("dom", None, None, None),
        P("dom", None),
        P("dom", None),
        P("dom", None),
        P("dom", None, None),
        P("dom"),
        P("dom"),
        P("dom"),
        P(),
        P(),
        P(),
        P(),
        P(),
    )
    out_specs = (P(), P(), P(), P(), P(), P("dom", None))
    return jax.shard_map(
        on_device, mesh=mesh, in_specs=in_specs, out_specs=out_specs, check_vma=False
    )
```

```python
import functools

import jax
import jax.numpy as jnp
from jax import lax
from jax.experimental import pallas as pl
from jax.experimental.pallas import tpu as pltpu
from jax.sharding import PartitionSpec as P

drift_rate = 0.5
LANES = 128
F32 = jnp.float32
BF16 = jnp.bfloat16
I32 = jnp.int32


def dot_nn(a, b):
    return lax.dot_general(a, b, (((1,), (0,)), ((), ())), preferred_element_type=F32)


def dot_nt(a, b):
    return lax.dot_general(a, b, (((1,), (1,)), ((), ())), preferred_element_type=F32)


def dot_tn(a, b):
    return lax.dot_general(a, b, (((0,), (0,)), ((), ())), preferred_element_type=F32)


def iota(shape, dim):
    return lax.broadcasted_iota(I32, shape, dim)


on_chip = pltpu.VMEM


def keep(x):
    return pltpu.with_memory_space_constraint(x, pltpu.VMEM)


def off_chip(x):
    return pltpu.with_memory_space_constraint(x, pltpu.HBM)


def params(n_grid=0, mib=20):
    kw = {} if n_grid == 0 else {"dimension_semantics": ("arbitrary",) * n_grid}
    return pltpu.CompilerParams(vmem_limit_bytes=mib << 20, **kw)


def pack_kernel(n, cap, _, hub_ref, mir_ref, link_ref, out_ref, place_ref):
    hubs, width = hub_ref.shape
    mirrors, links = link_ref.shape[0], link_ref.shape[1]
    dest = iota((n, hubs), 0)
    present = jnp.zeros((n, hubs), F32)
    for j in range(mirrors):
        present = present + jnp.where(mir_ref[j : j + 1, :] == dest, 1.0, 0.0)
    before = jnp.where(iota((hubs, hubs), 0) < iota((hubs, hubs), 1), 1.0, 0.0)
    rank = dot_nn(present.astype(BF16), before.astype(BF16))
    rank = jnp.where(present > 0.0, rank, 9999.0).astype(I32)
    place = jnp.where(rank[:, None, :] == iota((n, cap, hubs), 1), 1.0, 0.0)
    flat_place = place.reshape(n * cap, hubs).astype(BF16)
    place_ref[...] = flat_place
    rows = dot_nn(flat_place, hub_ref[...])
    out_ref[:, 0:cap, :] = rows.reshape(n, cap, width).astype(BF16)
    dest3 = iota((n, links, hubs), 0)
    ends = jnp.zeros((n, links, hubs), I32)
    for j in range(mirrors):
        ends = ends + jnp.where(mir_ref[j : j + 1, :][None] == dest3, link_ref[j][None], 0)
    high = ((ends >> 7) + 1).astype(F32)
    low = (ends & 127).astype(F32)
    both = jnp.concatenate([high, low], axis=1).astype(BF16)
    packed = lax.dot_general(
        both, place.astype(BF16), (((2,), (2,)), ((0,), (0,))), preferred_element_type=F32
    )
    rows = 2 * links * cap // LANES
    lanes = [packed[:, q * rows : (q + 1) * rows, :] for q in range(LANES // cap)]
    out_ref[:, cap : cap + rows, :] = jnp.concatenate(lanes, axis=2).astype(BF16)


def to_row(block):
    eye = iota(block.shape, 0) == iota(block.shape, 1)
    return jnp.sum(jnp.where(eye, block, 0.0), axis=0, keepdims=True)


def to_column(row):
    eye = iota((LANES, LANES), 0) == iota((LANES, LANES), 1)
    return jnp.sum(jnp.where(eye, row, 0.0), axis=1, keepdims=True)


def turn(x):
    return x.astype(F32).T


def local_kernel(
    tiles, cols_ref, feats_ref, vals_ref, ws_ref, wn_ref, wc_ref, bias_ref,
    s_ref, ft_ref, mass_ref, w_ref, wct_ref, wcn_ref, biasb_ref, wide,
):
    step = pl.program_id(0)
    width = feats_ref.shape[1]
    blocks = wide.shape[0]
    hidden_rows = ws_ref.shape[1]
    classes = wc_ref.shape[0]
    class_rows = wct_ref.shape[0]

    @pl.when(step == 0)
    def _():
        def fill(b, carry):
            wide[b, :, 0:width] = feats_ref[pl.ds(pl.multiple_of(b * LANES, LANES), LANES), :]
            wide[b, :, width:] = jnp.ones((LANES, LANES), BF16)
            return carry

        lax.fori_loop(0, blocks, fill, 0, unroll=4)
        wct_ref[...] = jnp.zeros_like(wct_ref)
        wct_ref[0:classes, :] = wc_ref[...]
        for b in range(hidden_rows // LANES):
            at = slice(b * LANES, (b + 1) * LANES)
            w_ref[at, 0:width] = turn(ws_ref[:, at]).astype(BF16)
            w_ref[at, width:] = turn(wn_ref[:, at]).astype(BF16)
            wcn_ref[at, :] = turn(wct_ref[:, at]).astype(BF16)
            biasb_ref[at, :] = jnp.broadcast_to(to_column(bias_ref[b : b + 1, :]), (LANES, LANES))

    per_step = vals_ref.shape[0]
    parts = s_ref.shape[2] // LANES
    for r in range(per_step):
        block = step * per_step + r
        home, part = step * (per_step // parts) + r // parts, r % parts
        span = slice(part * LANES, (part + 1) * LANES)
        left = jnp.concatenate([vals_ref[r, k] for k in range(tiles)], axis=1)
        right = jnp.concatenate([wide[cols_ref[k, block]] for k in range(tiles)], axis=0)
        both = dot_nn(left, right)
        own = wide[block, :, 0:width].astype(F32).T
        s_ref[r // parts, :, span] = own + both[:, 0:width].T
        ft_ref[home, :, span] = own.astype(BF16)
        mass_ref[home, :, span] = to_row(both[:, width : width + LANES])


def lane_row(ref, step, parts):
    return jnp.concatenate([ref[pl.ds(step * parts + k, 1), :] for k in range(parts)], axis=1)


def fold_lanes(x):
    total = x[:, 0:LANES]
    for k in range(1, x.shape[1] // LANES):
        total = total + x[:, k * LANES : (k + 1) * LANES]
    return total


def forward_kernel(
    n, cap, links, classes, span,
    recv_ref, s_ref, ft_ref, mass_ref, label_ref, group_ref, mask_ref, w_ref, bias_ref, wc_ref,
    agg_ref, hid_ref, pmo_ref, m_ref, inv_ref, of_ref, sums_ref,
    src, word_of, value_of, loss_acc, count_acc,
):
    step = pl.program_id(0)
    slots = n * cap
    width = s_ref.shape[1]
    groups = loss_acc.shape[0]
    parts = span // LANES

    @pl.when(step == 0)
    def _():
        loss_acc[...] = jnp.zeros_like(loss_acc)
        count_acc[...] = jnp.zeros_like(count_acc)
        per = LANES // cap
        rows = 2 * links // per
        block_of = iota((1, 1, LANES), 2) // cap
        ends = recv_ref[:, cap : cap + rows, :].astype(F32).reshape(n // per, per, rows, LANES)
        ends = [ends[:, k] for k in range(per)]
        turned = [[pltpu.roll(e, t * cap, 2) if t else e for t in range(per)] for e in ends]
        values = []
        for q in range(per):
            value = jnp.zeros((n // per, rows, LANES), F32)
            for k in range(per):
                value = jnp.where(block_of == k, turned[k][(k - q) % per], value)
            values.append(value)
        ends = jnp.concatenate(values, axis=1)
        for b in range(slots // LANES):
            at = slice(b * LANES, (b + 1) * LANES)
            rows = recv_ref[b * per : (b + 1) * per, 0:cap, :].astype(F32).reshape(LANES, width)
            src[0:width, at] = rows.T.astype(BF16)
            target = ((ends[b, 0:links] - 1.0) * 128.0 + ends[b, links:]).astype(I32)
            word_of[:, at] = (target >> 7) * 16 + (target & 15)
            value_of[:, at] = jnp.left_shift(1, ((target >> 4) & 7) * 4)
        src[width:, :] = jnp.ones((16, slots), BF16)

    chunk = 256
    for c in range(slots // chunk):
        at = slice(c * chunk, (c + 1) * chunk)
        word = [jnp.broadcast_to(word_of[k : k + 1, at], (16, chunk)) for k in range(links)]
        value = [jnp.broadcast_to(value_of[k : k + 1, at], (16, chunk)) for k in range(links)]
        for b in range(parts):
            rows16 = iota((16, chunk), 0) + (step * parts + b) * 16
            fields = jnp.zeros((16, chunk), I32)
            for k in range(links):
                fields = fields + jnp.where(word[k] == rows16, value[k], 0)
            for f in range(8):
                first = b * LANES + f * 16
                count = (fields >> (4 * f)) & 15
                m_ref[0, first : first + 16, at] = count.astype(F32).astype(BF16)
    hub = dot_nt(src[...], m_ref[0])
    inverse = 1.0 / (1.0 + mass_ref[step] + hub[width : width + 1, :])
    inv_ref[step] = inverse
    agg_ref[step] = ((s_ref[0] + hub[0:width]) * inverse).astype(BF16)
    bias = jnp.concatenate([bias_ref[...]] * parts, axis=1)
    both = jnp.concatenate([ft_ref[step], agg_ref[step]], axis=0)
    pre = dot_nn(w_ref[...], both) + bias
    hidden = jnp.maximum(pre, 0.0).astype(BF16)
    hid_ref[step] = hidden
    logits = dot_nn(wc_ref[...], hidden)
    class_row = iota(logits.shape, 0)
    logits = jnp.where(class_row < classes, logits, -jnp.inf)
    top = jnp.max(logits, axis=0, keepdims=True)
    shifted = jnp.exp(logits - top)
    total = jnp.sum(shifted, axis=0, keepdims=True)
    mask = lane_row(mask_ref, step, parts).astype(F32)
    hot = class_row == lane_row(label_ref, step, parts)
    picked = jnp.sum(jnp.where(hot, logits, 0.0), axis=0, keepdims=True)
    loss = (top + jnp.log(total) - picked) * mask
    pmo_ref[step] = shifted * (mask / total) - jnp.where(hot, mask, 0.0)
    group_row = lane_row(group_ref, step, parts)
    of_ref[step] = group_row
    in_group = iota((groups, span), 0) == group_row
    loss_acc[...] += fold_lanes(jnp.where(in_group, loss, 0.0))
    count_acc[...] += fold_lanes(jnp.where(in_group, mask, 0.0))

    @pl.when(step == pl.num_programs(0) - 1)
    def _():
        sub, lane = iota((groups, LANES), 0), iota((groups, LANES), 1)
        loss_col = jnp.sum(loss_acc[...], axis=1, keepdims=True)
        count_col = jnp.sum(count_acc[...], axis=1, keepdims=True)
        both = jnp.where(lane == sub, loss_col, 0.0) + jnp.where(
            lane == sub + groups, count_col, 0.0
        )
        row = jnp.sum(both, axis=0, keepdims=True)
        sums_ref[...] = jnp.broadcast_to(row[None], sums_ref.shape)


def backward_kernel(
    span,
    me_ref, sums_ref, logw_ref, pmo_ref, hid_ref, ft_ref, agg_ref, inv_ref, group_ref, wc_ref, wn_ref,
    own_ref, pass_ref, obj_ref, dsum_ref,
    q_col, gw, gwc, gb, flat,
):
    step = pl.program_id(0)
    half, share = pass_ref.shape[0], pass_ref.shape[1]
    groups = logw_ref.shape[1]
    hidden_rows = gb.shape[0]
    class_rows = pmo_ref.shape[1]

    @pl.when(step == 0)
    def _():
        row = jnp.sum(sums_ref[...], axis=0)
        sub, lane = iota((groups, LANES), 0), iota((groups, LANES), 1)
        gsum = jnp.sum(jnp.where(lane == sub, row, 0.0), axis=1, keepdims=True)
        gcount = jnp.sum(jnp.where(lane == sub + groups, row, 0.0), axis=1, keepdims=True)
        sub, lane = iota((groups, groups), 0), iota((groups, groups), 1)
        logw = jnp.sum(jnp.where(lane == sub, logw_ref[...], 0.0), axis=1, keepdims=True)
        score = logw + drift_rate * gsum / (gcount + 1.0)
        e = jnp.exp(score - jnp.max(score, axis=0, keepdims=True))
        q = groups * (e / jnp.sum(e, axis=0, keepdims=True))
        obj_ref[0, 0] = jnp.sum(q * gsum)
        q_col[...] = jnp.broadcast_to(q, q_col.shape)
        gw[...] = jnp.zeros_like(gw)
        gwc[...] = jnp.zeros_like(gwc)
        gb[...] = jnp.zeros_like(gb)

    in_group = iota((groups, span), 0) == group_ref[step]
    weight = jnp.sum(jnp.where(in_group, q_col[:, 0:1], 0.0), axis=0, keepdims=True)
    dlogits = (pmo_ref[step] * weight).astype(BF16)
    hidden = hid_ref[step]
    gwc[...] += dot_nt(hidden, dlogits)
    dhidden = dot_nn(wc_ref[...], dlogits)
    live = hidden > 0
    gb[...] += fold_lanes(jnp.where(live, dhidden, 0.0))
    dpre = jnp.where(live, dhidden.astype(BF16), jnp.zeros_like(hidden))
    gw[...] += dot_nt(dpre, jnp.concatenate([ft_ref[step], agg_ref[step]], axis=0))
    dagg = dot_nn(wn_ref[...], dpre)
    dsum_ref[step] = (dagg * inv_ref[step]).astype(BF16)

    @pl.when(step == pl.num_programs(0) - 1)
    def _():
        row = 0
        for b in range(gw.shape[1] // LANES):
            flat[row : row + hidden_rows, :] = gw[:, b * LANES : (b + 1) * LANES]
            row += hidden_rows
        for b in range(hidden_rows // LANES):
            flat[row : row + class_rows, :] = gwc[b * LANES : (b + 1) * LANES, :].T
            row += class_rows
        flat[row:, :] = jnp.zeros((flat.shape[0] - row, LANES), F32)
        for b in range(hidden_rows // LANES):
            col = jnp.sum(gb[b * LANES : (b + 1) * LANES, :], axis=1, keepdims=True)
            flat[row + b : row + b + 1, :] = to_row(jnp.broadcast_to(col, (LANES, LANES)))
        core = me_ref[0] % 2
        for d in range(half):
            own_at = pl.multiple_of((2 * d + core) * share, 8)
            own_ref[d] = flat[pl.ds(own_at, share), :]
            pass_at = pl.multiple_of((2 * d + 1 - core) * share, 8)
            pass_ref[d] = flat[pl.ds(pass_at, share), :].astype(BF16)


def slot_kernel(dsum_ref, m_ref, place_ref, out_ref, turned_ref, slot):
    step = pl.program_id(0)
    n, cap = out_ref.shape[0], out_ref.shape[1]
    slots = n * cap

    @pl.when(step == 0)
    def _():
        slot[...] = jnp.zeros_like(slot)
        for b in range(slots // LANES):
            at = slice(b * LANES, (b + 1) * LANES)
            turned_ref[:, at] = turn(place_ref[at, :]).astype(BF16)

    total = slot[...]
    blocks = m_ref.shape[0]
    for k in range(blocks):
        total = total + dot_nn(dsum_ref[step * blocks + k], m_ref[k])
    slot[...] = total

    @pl.when(step == pl.num_programs(0) - 1)
    def _():
        per = LANES // cap
        for b in range(slots // LANES):
            rows = slot[:, b * LANES : (b + 1) * LANES].T
            out_ref[b * per : (b + 1) * per] = rows.reshape(per, cap, LANES).astype(BF16)


def pair_kernel(own_ref, recv_ref, out_ref):
    out_ref[...] = (own_ref[...] + recv_ref[...].astype(F32)).astype(BF16)


def reduce_kernel(recv_ref, slot_ref, out_ref):
    n, cap = slot_ref.shape[0], slot_ref.shape[1]
    part = out_ref.shape[1] - cap
    total = recv_ref[0].astype(F32)
    for d in range(1, recv_ref.shape[0]):
        total = total + recv_ref[d].astype(F32)
    halves = [total[0:part].astype(BF16), total[part:].astype(BF16)]
    out_ref[:, 0:cap, :] = slot_ref[...]
    for d in range(n):
        out_ref[d, cap:, :] = halves[d % 2]


def final_kernel(
    cap, me_ref, recv_ref, other_ref, place_ref, gws_ref, gwn_ref, gb_ref, gwc_ref, hub_ref, flat
):
    n, part, width = recv_ref.shape[0], recv_ref.shape[1] - cap, recv_ref.shape[2]
    rows = recv_ref[:, 0:cap, :].astype(F32).reshape(n * cap, width).astype(BF16)
    hub_ref[...] = dot_nn(place_ref[...], rows)
    even = me_ref[0] % 2 == 0
    for d in range(n):
        mine = recv_ref[d, cap:, :].astype(F32)
        other = other_ref[d, cap:, :].astype(F32)
        flat[2 * d * part : (2 * d + 1) * part, :] = jnp.where(even, mine, other)
        flat[(2 * d + 1) * part : (2 * d + 2) * part, :] = jnp.where(even, other, mine)
    hidden_rows = gws_ref.shape[1]
    classes = gwc_ref.shape[0]
    class_rows = -(-classes // 16) * 16
    row = 2 * hidden_rows
    for b in range(hidden_rows // LANES):
        at = slice(b * LANES, (b + 1) * LANES)
        gws_ref[:, at] = flat[b * LANES : (b + 1) * LANES, :].T
        gwn_ref[:, at] = flat[hidden_rows + b * LANES : hidden_rows + (b + 1) * LANES, :].T
        gwc_ref[:, at] = flat[row : row + classes, :]
        row += class_rows
    gb_ref[...] = flat[row : row + hidden_rows // LANES, :]


def exchange(x):
    return lax.all_to_all(x, "dom", split_axis=0, concat_axis=0, tiled=True)


def on_device(
    feats, adj_vals, adj_cols, hub_feats, hub_mirrors, hub_links, labels, groups, train_mask,
    w_self, w_neigh, bias, w_cls, group_logw,
):
    verts, width = feats.shape
    n = lax.axis_size("dom")
    hub_dev = hub_feats.shape[0]
    mirrors = hub_mirrors.shape[1]
    links = hub_links.shape[2]
    group_total = group_logw.shape[0]
    hidden_rows, classes = w_cls.shape
    class_rows = -(-classes // 16) * 16
    row_blocks, tiles = adj_cols.shape
    cap = min(hub_dev, max(2, 2 * hub_dev * mirrors // n))
    slots = n * cap
    any_space = pl.BlockSpec(memory_space=pltpu.VMEM)
    smem = pl.BlockSpec(memory_space=pltpu.SMEM)
    sds = jax.ShapeDtypeStruct

    link_rows = 2 * links * cap // LANES
    me = lax.axis_index("dom").reshape(1).astype(I32)
    packed, place = pl.pallas_call(
        functools.partial(pack_kernel, n, cap),
        name="pack",
        out_shape=(sds((n, cap + link_rows, width), BF16), sds((slots, hub_dev), BF16)),
        in_specs=[smem, any_space, any_space, any_space],
        out_specs=(any_space, any_space),
        compiler_params=params(),
    )(me, off_chip(hub_feats), off_chip(hub_mirrors.T), off_chip(hub_links.transpose(1, 2, 0)))
    recv = exchange(packed)

    parts = 8
    span = parts * LANES
    steps = row_blocks // parts
    per_step = parts
    whole = lambda *shape: pl.BlockSpec(shape, lambda i, *_: (0,) * len(shape))
    s_rows, f_turned, mass, w_turned, wc_turned, wc_rows, bias_wide = pl.pallas_call(
        functools.partial(local_kernel, tiles),
        name="local",
        grid_spec=pltpu.PrefetchScalarGridSpec(
            num_scalar_prefetch=1,
            grid=(row_blocks // per_step,),
            in_specs=[
                whole(verts, width),
                pl.BlockSpec((per_step, tiles, LANES, LANES), lambda i, *_: (i, 0, 0, 0)),
                whole(width, hidden_rows),
                whole(width, hidden_rows),
                whole(classes, hidden_rows),
                whole(hidden_rows // LANES, LANES),
            ],
            out_specs=[
                pl.BlockSpec((per_step // parts, width, span), lambda i, *_: (i, 0, 0))
            ]
            + [any_space] * 4
            + [whole(hidden_rows, class_rows), any_space],
            scratch_shapes=[pltpu.VMEM((row_blocks, LANES, 2 * width), BF16)],
        ),
        out_shape=(
            pltpu.HBM((steps, width, span), F32),
            on_chip((steps, width, span), BF16),
            on_chip((steps, 1, span), F32),
            on_chip((hidden_rows, 2 * width), BF16),
            on_chip((class_rows, hidden_rows), BF16),
            pltpu.HBM((hidden_rows, class_rows), BF16),
            on_chip((hidden_rows, LANES), F32),
        ),
        compiler_params=params(1, 16),
    )(
        off_chip(adj_cols.T), off_chip(feats), off_chip(adj_vals), off_chip(w_self), off_chip(w_neigh),
        off_chip(w_cls.T), off_chip(bias.reshape(hidden_rows // LANES, LANES)),
    )

    table = (verts // LANES, LANES)
    label_table, group_table = keep(labels.reshape(table)), keep(groups.reshape(table))
    mask_table = keep(train_mask.reshape(table))
    tile_at = pl.BlockSpec((1, span, slots), lambda i: (i, 0, 0))
    agg, hid, pmo, counts, inv, group_rows, sums = pl.pallas_call(
        functools.partial(forward_kernel, n, cap, links, classes, span),
        name="forward",
        grid=(steps,),
        in_specs=[any_space, pl.BlockSpec((1, width, span), lambda i: (i, 0, 0))]
        + [any_space] * 8,
        out_specs=[any_space] * 3 + [tile_at] + [any_space] * 3,
        out_shape=(
            on_chip((steps, width, span), BF16),
            on_chip((steps, hidden_rows, span), BF16),
            on_chip((steps, class_rows, span), F32),
            pltpu.HBM((steps, span, slots), BF16),
            on_chip((steps, 1, span), F32),
            on_chip((steps, 1, span), I32),
            sds((n, 1, LANES), F32),
        ),
        scratch_shapes=[
            pltpu.VMEM((width + 16, slots), BF16),
            pltpu.VMEM((links, slots), I32),
            pltpu.VMEM((links, slots), I32),
            pltpu.VMEM((group_total, LANES), F32),
            pltpu.VMEM((group_total, LANES), F32),
        ],
        compiler_params=params(1),
    )(
        keep(recv), off_chip(s_rows), keep(f_turned), keep(mass), label_table, group_table,
        mask_table, keep(w_turned), keep(bias_wide), keep(wc_turned),
    )
    all_sums = exchange(sums)

    grad_rows = hidden_rows // LANES * (2 * width + class_rows + 1)
    share = -(-grad_rows // (8 * n)) * 8
    half = n // 2
    own, passed, objective, dsum = pl.pallas_call(
        functools.partial(backward_kernel, span),
        name="backward",
        grid=(steps,),
        in_specs=[smem] + [any_space] * 10,
        out_specs=[any_space, any_space, smem, any_space],
        out_shape=(
            on_chip((half, share, LANES), F32), pltpu.HBM((half, share, LANES), BF16),
            sds((1, 1), F32), on_chip((steps, width, span), BF16),
        ),
        scratch_shapes=[
            pltpu.VMEM((group_total, LANES), F32),
            pltpu.VMEM((hidden_rows, 2 * width), F32),
            pltpu.VMEM((hidden_rows, class_rows), F32),
            pltpu.VMEM((hidden_rows, LANES), F32),
            pltpu.VMEM((n * share, LANES), F32),
        ],
        compiler_params=params(1),
    )(
        me, all_sums, group_logw.reshape(1, group_total), keep(pmo), keep(hid), keep(f_turned),
        keep(agg), keep(inv), keep(group_rows), keep(wc_rows), keep(w_neigh),
    )
    other = lax.ppermute(passed, "dom", [(i, i ^ 1) for i in range(n)])
    paired = pl.pallas_call(
        pair_kernel,
        name="pair",
        out_shape=pltpu.HBM((half, share, LANES), BF16),
        in_specs=[any_space, any_space],
        out_specs=any_space,
        compiler_params=params(),
    )(keep(own), keep(other))
    same_core = [list(range(core, n, 2)) for core in range(2)]
    answer = lax.all_to_all(
        paired, "dom", split_axis=0, concat_axis=0, tiled=True, axis_index_groups=same_core
    )

    blocks = 2 if steps % 2 == 0 else 1
    slot_grads, place_turned = pl.pallas_call(
        slot_kernel,
        name="slots",
        grid=(steps // blocks,),
        in_specs=[any_space, pl.BlockSpec((blocks, span, slots), lambda i: (i, 0, 0)), any_space],
        out_specs=[any_space] * 2,
        out_shape=(on_chip((n, cap, width), BF16), on_chip((hub_dev, slots), BF16)),
        scratch_shapes=[pltpu.VMEM((width, slots), F32)],
        compiler_params=params(1, 20),
    )(keep(dsum), off_chip(counts), keep(place))
    reduced = pl.pallas_call(
        reduce_kernel,
        name="reduce",
        out_shape=sds((n, cap + share // 2, LANES), BF16),
        in_specs=[any_space, any_space],
        out_specs=any_space,
        compiler_params=params(),
    )(keep(answer), keep(slot_grads))
    gathered = exchange(reduced)
    other_half = lax.ppermute(gathered, "dom", [(i, i ^ 1) for i in range(n)])
    grad_w_self, grad_w_neigh, grad_bias, grad_w_cls, hub_grad = pl.pallas_call(
        functools.partial(final_kernel, cap),
        name="final",
        out_shape=(
            sds((width, hidden_rows), F32),
            sds((width, hidden_rows), F32),
            sds((hidden_rows // LANES, LANES), F32),
            sds((classes, hidden_rows), F32),
            sds((hub_dev, width), F32),
        ),
        in_specs=[smem, any_space, any_space, any_space],
        out_specs=(any_space,) * 5,
        scratch_shapes=[pltpu.VMEM((n * share, LANES), F32)],
        compiler_params=params(),
    )(me, keep(gathered), keep(other_half), keep(place_turned))
    return (
        objective.reshape(()), grad_w_self, grad_w_neigh, grad_bias.reshape(hidden_rows),
        grad_w_cls.T, hub_grad,
    )


def solution(mesh):
    in_specs = (
        P("dom", None),
        P("dom", None, None, None),
        P("dom", None),
        P("dom", None),
        P("dom", None),
        P("dom", None, None),
        P("dom"),
        P("dom"),
        P("dom"),
        P(),
        P(),
        P(),
        P(),
        P(),
    )
    out_specs = (P(), P(), P(), P(), P(), P("dom", None))
    return jax.shard_map(
        on_device, mesh=mesh, in_specs=in_specs, out_specs=out_specs, check_vma=False
    )
```

```python
import functools

import jax
import jax.numpy as jnp
from jax import lax
from jax.experimental import pallas as pl
from jax.experimental.pallas import tpu as pltpu
from jax.sharding import PartitionSpec as P

drift_rate = 0.5
LANES = 128
F32 = jnp.float32
BF16 = jnp.bfloat16
I32 = jnp.int32


def dot_nn(a, b):
    return lax.dot_general(a, b, (((1,), (0,)), ((), ())), preferred_element_type=F32)


def dot_nt(a, b):
    return lax.dot_general(a, b, (((1,), (1,)), ((), ())), preferred_element_type=F32)


def dot_tn(a, b):
    return lax.dot_general(a, b, (((0,), (0,)), ((), ())), preferred_element_type=F32)


def iota(shape, dim):
    return lax.broadcasted_iota(I32, shape, dim)


on_chip = pltpu.VMEM


def keep(x):
    return pltpu.with_memory_space_constraint(x, pltpu.VMEM)


def off_chip(x):
    return pltpu.with_memory_space_constraint(x, pltpu.HBM)


def params(n_grid=0, mib=20):
    kw = {} if n_grid == 0 else {"dimension_semantics": ("arbitrary",) * n_grid}
    return pltpu.CompilerParams(vmem_limit_bytes=mib << 20, **kw)


def pack_kernel(n, cap, _, hub_ref, mir_ref, link_ref, out_ref, place_ref):
    hubs, width = hub_ref.shape
    mirrors, links = link_ref.shape[0], link_ref.shape[1]
    dest = iota((n, hubs), 0)
    present = jnp.zeros((n, hubs), F32)
    for j in range(mirrors):
        present = present + jnp.where(mir_ref[j : j + 1, :] == dest, 1.0, 0.0)
    before = jnp.where(iota((hubs, hubs), 0) < iota((hubs, hubs), 1), 1.0, 0.0)
    rank = dot_nn(present.astype(BF16), before.astype(BF16))
    rank = jnp.where(present > 0.0, rank, 9999.0).astype(I32)
    place = jnp.where(rank[:, None, :] == iota((n, cap, hubs), 1), 1.0, 0.0)
    flat_place = place.reshape(n * cap, hubs).astype(BF16)
    place_ref[...] = flat_place
    rows = dot_nn(flat_place, hub_ref[...])
    out_ref[:, 0:cap, :] = rows.reshape(n, cap, width).astype(BF16)
    dest3 = iota((n, links, hubs), 0)
    ends = jnp.zeros((n, links, hubs), I32)
    for j in range(mirrors):
        ends = ends + jnp.where(mir_ref[j : j + 1, :][None] == dest3, link_ref[j][None], 0)
    high = ((ends >> 7) + 1).astype(F32)
    low = (ends & 127).astype(F32)
    both = jnp.concatenate([high, low], axis=1).astype(BF16)
    packed = lax.dot_general(
        both, place.astype(BF16), (((2,), (2,)), ((0,), (0,))), preferred_element_type=F32
    )
    rows = 2 * links * cap // LANES
    lanes = [packed[:, q * rows : (q + 1) * rows, :] for q in range(LANES // cap)]
    out_ref[:, cap : cap + rows, :] = jnp.concatenate(lanes, axis=2).astype(BF16)


def to_row(block):
    eye = iota(block.shape, 0) == iota(block.shape, 1)
    return jnp.sum(jnp.where(eye, block, 0.0), axis=0, keepdims=True)


def to_column(row):
    eye = iota((LANES, LANES), 0) == iota((LANES, LANES), 1)
    return jnp.sum(jnp.where(eye, row, 0.0), axis=1, keepdims=True)


def turn(x):
    return x.astype(F32).T


def local_kernel(
    tiles, cols_ref, feats_ref, vals_ref, ws_ref, wn_ref, wc_ref, bias_ref,
    s_ref, ft_ref, mass_ref, w_ref, wct_ref, wcn_ref, biasb_ref, wide,
):
    step = pl.program_id(0)
    width = feats_ref.shape[1]
    blocks = wide.shape[0]
    hidden_rows = ws_ref.shape[1]
    classes = wc_ref.shape[0]
    class_rows = wct_ref.shape[0]

    @pl.when(step == 0)
    def _():
        def fill(b, carry):
            wide[b, :, 0:width] = feats_ref[pl.ds(pl.multiple_of(b * LANES, LANES), LANES), :]
            wide[b, :, width:] = jnp.ones((LANES, LANES), BF16)
            return carry

        lax.fori_loop(0, blocks, fill, 0, unroll=4)
        wct_ref[...] = jnp.zeros_like(wct_ref)
        wct_ref[0:classes, :] = wc_ref[...]
        for b in range(hidden_rows // LANES):
            at = slice(b * LANES, (b + 1) * LANES)
            w_ref[at, 0:width] = turn(ws_ref[:, at]).astype(BF16)
            w_ref[at, width:] = turn(wn_ref[:, at]).astype(BF16)
            wcn_ref[at, :] = turn(wct_ref[:, at]).astype(BF16)
            biasb_ref[at, :] = jnp.broadcast_to(to_column(bias_ref[b : b + 1, :]), (LANES, LANES))

    per_step = vals_ref.shape[0]
    parts = s_ref.shape[2] // LANES
    for r in range(per_step):
        block = step * per_step + r
        home, part = step * (per_step // parts) + r // parts, r % parts
        span = slice(part * LANES, (part + 1) * LANES)
        left = jnp.concatenate([vals_ref[r, k] for k in range(tiles)], axis=1)
        right = jnp.concatenate([wide[cols_ref[k, block]] for k in range(tiles)], axis=0)
        both = dot_nn(left, right)
        own = wide[block, :, 0:width].astype(F32).T
        s_ref[r // parts, :, span] = own + both[:, 0:width].T
        ft_ref[home, :, span] = own.astype(BF16)
        mass_ref[home, :, span] = to_row(both[:, width : width + LANES])


def lane_row(ref, step, parts):
    return jnp.concatenate([ref[pl.ds(step * parts + k, 1), :] for k in range(parts)], axis=1)


def fold_lanes(x):
    total = x[:, 0:LANES]
    for k in range(1, x.shape[1] // LANES):
        total = total + x[:, k * LANES : (k + 1) * LANES]
    return total


def forward_kernel(
    n, cap, links, classes, span,
    recv_ref, s_ref, ft_ref, mass_ref, label_ref, group_ref, mask_ref, w_ref, bias_ref, wc_ref,
    agg_ref, hid_ref, pmo_ref, m_ref, inv_ref, of_ref, sums_ref,
    src, word_of, value_of, loss_acc, count_acc,
):
    step = pl.program_id(0)
    slots = n * cap
    width = s_ref.shape[1]
    groups = loss_acc.shape[0]
    parts = span // LANES

    @pl.when(step == 0)
    def _():
        loss_acc[...] = jnp.zeros_like(loss_acc)
        count_acc[...] = jnp.zeros_like(count_acc)
        per = LANES // cap
        rows = 2 * links // per
        block_of = iota((1, 1, LANES), 2) // cap
        ends = recv_ref[:, cap : cap + rows, :].astype(F32).reshape(n // per, per, rows, LANES)
        ends = [ends[:, k] for k in range(per)]
        turned = [[pltpu.roll(e, t * cap, 2) if t else e for t in range(per)] for e in ends]
        values = []
        for q in range(per):
            value = jnp.zeros((n // per, rows, LANES), F32)
            for k in range(per):
                value = jnp.where(block_of == k, turned[k][(k - q) % per], value)
            values.append(value)
        ends = jnp.concatenate(values, axis=1)
        for b in range(slots // LANES):
            at = slice(b * LANES, (b + 1) * LANES)
            rows = recv_ref[b * per : (b + 1) * per, 0:cap, :].astype(F32).reshape(LANES, width)
            src[0:width, at] = rows.T.astype(BF16)
            target = ((ends[b, 0:links] - 1.0) * 128.0 + ends[b, links:]).astype(I32)
            word_of[:, at] = (target >> 7) * 16 + (target & 15)
            value_of[:, at] = jnp.left_shift(1, ((target >> 4) & 7) * 4)
        src[width:, :] = jnp.ones((16, slots), BF16)

    chunk = 512
    for c in range(slots // chunk):
        at = slice(c * chunk, (c + 1) * chunk)
        word = [jnp.broadcast_to(word_of[k : k + 1, at], (16, chunk)) for k in range(links)]
        value = [jnp.broadcast_to(value_of[k : k + 1, at], (16, chunk)) for k in range(links)]
        for b in range(parts):
            rows16 = iota((16, chunk), 0) + (step * parts + b) * 16
            fields = jnp.zeros((16, chunk), I32)
            for k in range(links):
                fields = fields + jnp.where(word[k] == rows16, value[k], 0)
            for f in range(8):
                first = b * LANES + f * 16
                count = (fields >> (4 * f)) & 15
                m_ref[0, first : first + 16, at] = count.astype(F32).astype(BF16)
    hub = dot_nt(src[...], m_ref[0])
    inverse = 1.0 / (1.0 + mass_ref[step] + hub[width : width + 1, :])
    inv_ref[step] = inverse
    agg_ref[step] = ((s_ref[0] + hub[0:width]) * inverse).astype(BF16)
    bias = jnp.concatenate([bias_ref[...]] * parts, axis=1)
    both = jnp.concatenate([ft_ref[step], agg_ref[step]], axis=0)
    pre = dot_nn(w_ref[...], both) + bias
    hidden = jnp.maximum(pre, 0.0).astype(BF16)
    hid_ref[step] = hidden
    logits = dot_nn(wc_ref[...], hidden)
    class_row = iota(logits.shape, 0)
    logits = jnp.where(class_row < classes, logits, -jnp.inf)
    top = jnp.max(logits, axis=0, keepdims=True)
    shifted = jnp.exp(logits - top)
    total = jnp.sum(shifted, axis=0, keepdims=True)
    mask = lane_row(mask_ref, step, parts).astype(F32)
    hot = class_row == lane_row(label_ref, step, parts)
    picked = jnp.sum(jnp.where(hot, logits, 0.0), axis=0, keepdims=True)
    loss = (top + jnp.log(total) - picked) * mask
    pmo_ref[step] = shifted * (mask / total) - jnp.where(hot, mask, 0.0)
    group_row = lane_row(group_ref, step, parts)
    of_ref[step] = group_row
    in_group = iota((groups, span), 0) == group_row
    loss_acc[...] += fold_lanes(jnp.where(in_group, loss, 0.0))
    count_acc[...] += fold_lanes(jnp.where(in_group, mask, 0.0))

    @pl.when(step == pl.num_programs(0) - 1)
    def _():
        sub, lane = iota((groups, LANES), 0), iota((groups, LANES), 1)
        loss_col = jnp.sum(loss_acc[...], axis=1, keepdims=True)
        count_col = jnp.sum(count_acc[...], axis=1, keepdims=True)
        both = jnp.where(lane == sub, loss_col, 0.0) + jnp.where(
            lane == sub + groups, count_col, 0.0
        )
        row = jnp.sum(both, axis=0, keepdims=True)
        sums_ref[...] = jnp.broadcast_to(row[None], sums_ref.shape)


def backward_kernel(
    span,
    me_ref, sums_ref, logw_ref, pmo_ref, hid_ref, ft_ref, agg_ref, inv_ref, group_ref, wc_ref, wn_ref,
    own_ref, pass_ref, obj_ref, dsum_ref,
    q_col, gw, gwc, gb, flat,
):
    step = pl.program_id(0)
    half, share = pass_ref.shape[0], pass_ref.shape[1]
    groups = logw_ref.shape[1]
    hidden_rows = gb.shape[0]
    class_rows = pmo_ref.shape[1]

    @pl.when(step == 0)
    def _():
        row = jnp.sum(sums_ref[...], axis=0)
        sub, lane = iota((groups, LANES), 0), iota((groups, LANES), 1)
        gsum = jnp.sum(jnp.where(lane == sub, row, 0.0), axis=1, keepdims=True)
        gcount = jnp.sum(jnp.where(lane == sub + groups, row, 0.0), axis=1, keepdims=True)
        sub, lane = iota((groups, groups), 0), iota((groups, groups), 1)
        logw = jnp.sum(jnp.where(lane == sub, logw_ref[...], 0.0), axis=1, keepdims=True)
        score = logw + drift_rate * gsum / (gcount + 1.0)
        e = jnp.exp(score - jnp.max(score, axis=0, keepdims=True))
        q = groups * (e / jnp.sum(e, axis=0, keepdims=True))
        obj_ref[0, 0] = jnp.sum(q * gsum)
        q_col[...] = jnp.broadcast_to(q, q_col.shape)
        gw[...] = jnp.zeros_like(gw)
        gwc[...] = jnp.zeros_like(gwc)
        gb[...] = jnp.zeros_like(gb)

    in_group = iota((groups, span), 0) == group_ref[step]
    weight = jnp.sum(jnp.where(in_group, q_col[:, 0:1], 0.0), axis=0, keepdims=True)
    dlogits = (pmo_ref[step] * weight).astype(BF16)
    hidden = hid_ref[step]
    gwc[...] += dot_nt(hidden, dlogits)
    dhidden = dot_nn(wc_ref[...], dlogits)
    live = hidden > 0
    gb[...] += fold_lanes(jnp.where(live, dhidden, 0.0))
    dpre = jnp.where(live, dhidden.astype(BF16), jnp.zeros_like(hidden))
    gw[...] += dot_nt(dpre, jnp.concatenate([ft_ref[step], agg_ref[step]], axis=0))
    dagg = dot_nn(wn_ref[...], dpre)
    dsum_ref[step] = (dagg * inv_ref[step]).astype(BF16)

    @pl.when(step == pl.num_programs(0) - 1)
    def _():
        row = 0
        for b in range(gw.shape[1] // LANES):
            flat[row : row + hidden_rows, :] = gw[:, b * LANES : (b + 1) * LANES]
            row += hidden_rows
        for b in range(hidden_rows // LANES):
            flat[row : row + class_rows, :] = gwc[b * LANES : (b + 1) * LANES, :].T
            row += class_rows
        flat[row:, :] = jnp.zeros((flat.shape[0] - row, LANES), F32)
        for b in range(hidden_rows // LANES):
            col = jnp.sum(gb[b * LANES : (b + 1) * LANES, :], axis=1, keepdims=True)
            flat[row + b : row + b + 1, :] = to_row(jnp.broadcast_to(col, (LANES, LANES)))
        core = me_ref[0] % 2
        for d in range(half):
            own_at = pl.multiple_of((2 * d + core) * share, 8)
            own_ref[d] = flat[pl.ds(own_at, share), :]
            pass_at = pl.multiple_of((2 * d + 1 - core) * share, 8)
            pass_ref[d] = flat[pl.ds(pass_at, share), :].astype(BF16)


def slot_kernel(dsum_ref, m_ref, place_ref, out_ref, turned_ref, slot):
    step = pl.program_id(0)
    n, cap = out_ref.shape[0], out_ref.shape[1]
    slots = n * cap

    @pl.when(step == 0)
    def _():
        slot[...] = jnp.zeros_like(slot)
        for b in range(slots // LANES):
            at = slice(b * LANES, (b + 1) * LANES)
            turned_ref[:, at] = turn(place_ref[at, :]).astype(BF16)

    total = slot[...]
    blocks = m_ref.shape[0]
    for k in range(blocks):
        total = total + dot_nn(dsum_ref[step * blocks + k], m_ref[k])
    slot[...] = total

    @pl.when(step == pl.num_programs(0) - 1)
    def _():
        per = LANES // cap
        for b in range(slots // LANES):
            rows = slot[:, b * LANES : (b + 1) * LANES].T
            out_ref[b * per : (b + 1) * per] = rows.reshape(per, cap, LANES).astype(BF16)


def pair_kernel(own_ref, recv_ref, out_ref):
    out_ref[...] = (own_ref[...] + recv_ref[...].astype(F32)).astype(BF16)


def reduce_kernel(recv_ref, slot_ref, out_ref):
    n, cap = slot_ref.shape[0], slot_ref.shape[1]
    part = out_ref.shape[1] - cap
    total = recv_ref[0].astype(F32)
    for d in range(1, recv_ref.shape[0]):
        total = total + recv_ref[d].astype(F32)
    halves = [total[0:part].astype(BF16), total[part:].astype(BF16)]
    out_ref[:, 0:cap, :] = slot_ref[...]
    for d in range(n):
        out_ref[d, cap:, :] = halves[d % 2]


def final_kernel(
    cap, me_ref, recv_ref, other_ref, place_ref, gws_ref, gwn_ref, gb_ref, gwc_ref, hub_ref, flat
):
    n, part, width = recv_ref.shape[0], recv_ref.shape[1] - cap, recv_ref.shape[2]
    rows = recv_ref[:, 0:cap, :].astype(F32).reshape(n * cap, width).astype(BF16)
    hub_ref[...] = dot_nn(place_ref[...], rows)
    even = me_ref[0] % 2 == 0
    for d in range(n):
        mine = recv_ref[d, cap:, :].astype(F32)
        other = other_ref[d, cap:, :].astype(F32)
        flat[2 * d * part : (2 * d + 1) * part, :] = jnp.where(even, mine, other)
        flat[(2 * d + 1) * part : (2 * d + 2) * part, :] = jnp.where(even, other, mine)
    hidden_rows = gws_ref.shape[1]
    classes = gwc_ref.shape[0]
    class_rows = -(-classes // 16) * 16
    row = 2 * hidden_rows
    for b in range(hidden_rows // LANES):
        at = slice(b * LANES, (b + 1) * LANES)
        gws_ref[:, at] = flat[b * LANES : (b + 1) * LANES, :].T
        gwn_ref[:, at] = flat[hidden_rows + b * LANES : hidden_rows + (b + 1) * LANES, :].T
        gwc_ref[:, at] = flat[row : row + classes, :]
        row += class_rows
    gb_ref[...] = flat[row : row + hidden_rows // LANES, :]


def exchange(x):
    return lax.all_to_all(x, "dom", split_axis=0, concat_axis=0, tiled=True)


def on_device(
    feats, adj_vals, adj_cols, hub_feats, hub_mirrors, hub_links, labels, groups, train_mask,
    w_self, w_neigh, bias, w_cls, group_logw,
):
    verts, width = feats.shape
    n = lax.axis_size("dom")
    hub_dev = hub_feats.shape[0]
    mirrors = hub_mirrors.shape[1]
    links = hub_links.shape[2]
    group_total = group_logw.shape[0]
    hidden_rows, classes = w_cls.shape
    class_rows = -(-classes // 16) * 16
    row_blocks, tiles = adj_cols.shape
    cap = min(hub_dev, max(2, 2 * hub_dev * mirrors // n))
    slots = n * cap
    any_space = pl.BlockSpec(memory_space=pltpu.VMEM)
    smem = pl.BlockSpec(memory_space=pltpu.SMEM)
    sds = jax.ShapeDtypeStruct

    link_rows = 2 * links * cap // LANES
    me = lax.axis_index("dom").reshape(1).astype(I32)
    packed, place = pl.pallas_call(
        functools.partial(pack_kernel, n, cap),
        name="pack",
        out_shape=(sds((n, cap + link_rows, width), BF16), sds((slots, hub_dev), BF16)),
        in_specs=[smem, any_space, any_space, any_space],
        out_specs=(any_space, any_space),
        compiler_params=params(),
    )(me, off_chip(hub_feats), off_chip(hub_mirrors.T), off_chip(hub_links.transpose(1, 2, 0)))
    recv = exchange(packed)

    parts = 8
    span = parts * LANES
    steps = row_blocks // parts
    per_step = parts
    whole = lambda *shape: pl.BlockSpec(shape, lambda i, *_: (0,) * len(shape))
    s_rows, f_turned, mass, w_turned, wc_turned, wc_rows, bias_wide = pl.pallas_call(
        functools.partial(local_kernel, tiles),
        name="local",
        grid_spec=pltpu.PrefetchScalarGridSpec(
            num_scalar_prefetch=1,
            grid=(row_blocks // per_step,),
            in_specs=[
                whole(verts, width),
                pl.BlockSpec((per_step, tiles, LANES, LANES), lambda i, *_: (i, 0, 0, 0)),
                whole(width, hidden_rows),
                whole(width, hidden_rows),
                whole(classes, hidden_rows),
                whole(hidden_rows // LANES, LANES),
            ],
            out_specs=[
                pl.BlockSpec((per_step // parts, width, span), lambda i, *_: (i, 0, 0))
            ]
            + [any_space] * 4
            + [whole(hidden_rows, class_rows), any_space],
            scratch_shapes=[pltpu.VMEM((row_blocks, LANES, 2 * width), BF16)],
        ),
        out_shape=(
            pltpu.HBM((steps, width, span), F32),
            on_chip((steps, width, span), BF16),
            on_chip((steps, 1, span), F32),
            on_chip((hidden_rows, 2 * width), BF16),
            on_chip((class_rows, hidden_rows), BF16),
            pltpu.HBM((hidden_rows, class_rows), BF16),
            on_chip((hidden_rows, LANES), F32),
        ),
        compiler_params=params(1, 16),
    )(
        off_chip(adj_cols.T), off_chip(feats), off_chip(adj_vals), off_chip(w_self), off_chip(w_neigh),
        off_chip(w_cls.T), off_chip(bias.reshape(hidden_rows // LANES, LANES)),
    )

    table = (verts // LANES, LANES)
    label_table, group_table = keep(labels.reshape(table)), keep(groups.reshape(table))
    mask_table = keep(train_mask.reshape(table))
    tile_at = pl.BlockSpec((1, span, slots), lambda i: (i, 0, 0))
    agg, hid, pmo, counts, inv, group_rows, sums = pl.pallas_call(
        functools.partial(forward_kernel, n, cap, links, classes, span),
        name="forward",
        grid=(steps,),
        in_specs=[any_space, pl.BlockSpec((1, width, span), lambda i: (i, 0, 0))]
        + [any_space] * 8,
        out_specs=[any_space] * 3 + [tile_at] + [any_space] * 3,
        out_shape=(
            on_chip((steps, width, span), BF16),
            on_chip((steps, hidden_rows, span), BF16),
            on_chip((steps, class_rows, span), F32),
            pltpu.HBM((steps, span, slots), BF16),
            on_chip((steps, 1, span), F32),
            on_chip((steps, 1, span), I32),
            sds((n, 1, LANES), F32),
        ),
        scratch_shapes=[
            pltpu.VMEM((width + 16, slots), BF16),
            pltpu.VMEM((links, slots), I32),
            pltpu.VMEM((links, slots), I32),
            pltpu.VMEM((group_total, LANES), F32),
            pltpu.VMEM((group_total, LANES), F32),
        ],
        compiler_params=params(1),
    )(
        keep(recv), off_chip(s_rows), keep(f_turned), keep(mass), label_table, group_table,
        mask_table, keep(w_turned), keep(bias_wide), keep(wc_turned),
    )
    all_sums = exchange(sums)

    grad_rows = hidden_rows // LANES * (2 * width + class_rows + 1)
    share = -(-grad_rows // (8 * n)) * 8
    half = n // 2
    own, passed, objective, dsum = pl.pallas_call(
        functools.partial(backward_kernel, span),
        name="backward",
        grid=(steps,),
        in_specs=[smem] + [any_space] * 10,
        out_specs=[any_space, any_space, smem, any_space],
        out_shape=(
            on_chip((half, share, LANES), F32), pltpu.HBM((half, share, LANES), BF16),
            sds((1, 1), F32), on_chip((steps, width, span), BF16),
        ),
        scratch_shapes=[
            pltpu.VMEM((group_total, LANES), F32),
            pltpu.VMEM((hidden_rows, 2 * width), F32),
            pltpu.VMEM((hidden_rows, class_rows), F32),
            pltpu.VMEM((hidden_rows, LANES), F32),
            pltpu.VMEM((n * share, LANES), F32),
        ],
        compiler_params=params(1),
    )(
        me, all_sums, group_logw.reshape(1, group_total), keep(pmo), keep(hid), keep(f_turned),
        keep(agg), keep(inv), keep(group_rows), keep(wc_rows), keep(w_neigh),
    )
    other = lax.ppermute(passed, "dom", [(i, i ^ 1) for i in range(n)])
    paired = pl.pallas_call(
        pair_kernel,
        name="pair",
        out_shape=pltpu.HBM((half, share, LANES), BF16),
        in_specs=[any_space, any_space],
        out_specs=any_space,
        compiler_params=params(),
    )(keep(own), keep(other))
    same_core = [list(range(core, n, 2)) for core in range(2)]
    answer = lax.all_to_all(
        paired, "dom", split_axis=0, concat_axis=0, tiled=True, axis_index_groups=same_core
    )

    blocks = 2 if steps % 2 == 0 else 1
    slot_grads, place_turned = pl.pallas_call(
        slot_kernel,
        name="slots",
        grid=(steps // blocks,),
        in_specs=[any_space, pl.BlockSpec((blocks, span, slots), lambda i: (i, 0, 0)), any_space],
        out_specs=[any_space] * 2,
        out_shape=(on_chip((n, cap, width), BF16), on_chip((hub_dev, slots), BF16)),
        scratch_shapes=[pltpu.VMEM((width, slots), F32)],
        compiler_params=params(1, 20),
    )(keep(dsum), off_chip(counts), keep(place))
    reduced = pl.pallas_call(
        reduce_kernel,
        name="reduce",
        out_shape=sds((n, cap + share // 2, LANES), BF16),
        in_specs=[any_space, any_space],
        out_specs=any_space,
        compiler_params=params(),
    )(keep(answer), keep(slot_grads))
    gathered = exchange(reduced)
    other_half = lax.ppermute(gathered, "dom", [(i, i ^ 1) for i in range(n)])
    grad_w_self, grad_w_neigh, grad_bias, grad_w_cls, hub_grad = pl.pallas_call(
        functools.partial(final_kernel, cap),
        name="final",
        out_shape=(
            sds((width, hidden_rows), F32),
            sds((width, hidden_rows), F32),
            sds((hidden_rows // LANES, LANES), F32),
            sds((classes, hidden_rows), F32),
            sds((hub_dev, width), F32),
        ),
        in_specs=[smem, any_space, any_space, any_space],
        out_specs=(any_space,) * 5,
        scratch_shapes=[pltpu.VMEM((n * share, LANES), F32)],
        compiler_params=params(),
    )(me, keep(gathered), keep(other_half), keep(place_turned))
    return (
        objective.reshape(()), grad_w_self, grad_w_neigh, grad_bias.reshape(hidden_rows),
        grad_w_cls.T, hub_grad,
    )


def solution(mesh):
    in_specs = (
        P("dom", None),
        P("dom", None, None, None),
        P("dom", None),
        P("dom", None),
        P("dom", None),
        P("dom", None, None),
        P("dom"),
        P("dom"),
        P("dom"),
        P(),
        P(),
        P(),
        P(),
        P(),
    )
    out_specs = (P(), P(), P(), P(), P(), P("dom", None))
    return jax.shard_map(
        on_device, mesh=mesh, in_specs=in_specs, out_specs=out_specs, check_vma=False
    )
```
